256 devices in a mesh: sec: 16 (over y, z_lo, core), strip: 16 (over x, z_hi).
Axes of the slice: x: 4, y: 4, z: 8 (z_hi: 4, z_lo: 2; z = z_hi * 2 + z_lo), core: 2. Of those that a mesh axis runs over, the one named last changes fastest.
Arguments:
- positions: float32 [48, 2, 512, 1024], P('sec', None, 'strip'), may hold values from -6 to 6
- velocity: float32 [48, 2, 512, 1024], P('sec', None, 'strip'), may hold values from -4 to 4
- spring_class: int32 [48, 2, 512, 1024], P('sec', None, 'strip'), may hold values from 0 to 7
- match_shift: int32 [48, 2, 64, 8], P('sec', None, 'strip'), may hold values from -3 to 3
- fixed: int32 [48], P('sec'), may hold values 0 or 1
- class_stiffness: float32 [8], replicated, may hold values from 0.1 to 1
- cross_stiffness: float32 [2], replicated, may hold values from 0.2 to 1
Outputs:
- new_positions: float32 [48, 2, 512, 1024], P('sec', None, 'strip')
- new_velocity: float32 [48, 2, 512, 1024], P('sec', None, 'strip')
The draws below stay inside these ranges and needn't reach their ends.
All inputs are finite; a program needn't handle non-finite values. No bound on the sum of `fixed` on one device may be relied on, other than what follows from the above.
Results may differ from the reference program's by a relative error of at most 0.0003.
Values sent between devices are 32-bit elements; how exact they have to be, the bound alone decides.
A program may use at most 64 MiB of HBM per device.

```python
import math
import jax
import jax.numpy as jnp
from jax import lax

HEIGHT = 512
WIDTH = 1024
BLOCK_ROWS = 8
BLOCK_COLS = 128
MAX_SHIFT = 3
CLASSES = 8
STEPS = 2
SECTIONS = 48


def place_ends(entries, rng, least, high):
    dims = entries.shape
    index_at = [jax.random.randint(jax.random.fold_in(rng, axis), (), 0, dims[axis]) for axis in range(len(dims))]
    entries = entries.at[tuple(index_at)].set(least)
    longest = dims.index(max(dims))
    index_at[longest] = (index_at[longest] + 1) % dims[longest]
    return entries.at[tuple(index_at)].set(high)


def steps_of(stream_key, extent, pieces, low, largest):
    def one(dim, blocks):
        heights = jax.random.uniform(jax.random.fold_in(jax.random.fold_in(stream_key, 6), dim), (blocks,), jnp.float32, low / len(pieces), largest / len(pieces))
        return jnp.repeat(jnp.exp(heights), extent[dim] // blocks).reshape((-1,) + (1,) * (len(extent) - dim - 1))

    level = one(*pieces[0])
    for cut in pieces[1:]:
        level = level * one(*cut)
    return level


def noise(rng, dims, scale, bound, shards=(), kind=jnp.bfloat16):
    drawn = scale * jax.random.normal(rng, dims, jnp.float32)
    if shards:
        drawn = drawn * steps_of(rng, dims, shards, -0.22, 0.18)
    return jnp.clip(drawn, -bound, bound).astype(kind)


def setup_inputs(seed: int = 0) -> dict:
    arg_keys = jax.random.split(jax.random.key(seed), 8)
    return {
        "positions": noise(arg_keys[0], (SECTIONS, 2, HEIGHT, WIDTH), 1.0, 6.0, ((0, 16), (2, 16)), jnp.float32),
        "velocity": noise(arg_keys[1], (SECTIONS, 2, HEIGHT, WIDTH), 0.5, 4.0, ((0, 16), (2, 16)), jnp.float32),
        "spring_class": place_ends(jax.random.randint(arg_keys[2], (SECTIONS, 2, HEIGHT, WIDTH), 0, CLASSES), jax.random.fold_in(arg_keys[2], 1), 0, CLASSES - 1).astype(jnp.int32),
        "match_shift": place_ends(jax.random.randint(arg_keys[3], (SECTIONS, 2, HEIGHT // BLOCK_ROWS, WIDTH // BLOCK_COLS), 0 - MAX_SHIFT, MAX_SHIFT + 1), jax.random.fold_in(arg_keys[3], 1), 0 - MAX_SHIFT, MAX_SHIFT).astype(jnp.int32),
        "fixed": place_ends((jax.random.randint(arg_keys[4], (SECTIONS,), 0, 4) < 1).astype(jnp.int32), jax.random.fold_in(arg_keys[4], 1), 0, 1),
        "class_stiffness": jnp.clip(jnp.exp(jax.random.uniform(arg_keys[5], (CLASSES,), jnp.float32, math.log(0.1), math.log(1.0))), 0.1, 1.0),
        "cross_stiffness": jnp.clip(jnp.exp(jax.random.uniform(arg_keys[6], (2,), jnp.float32, math.log(0.2), math.log(1.0))), 0.2, 1.0),
    }


damping_rate = 0.9
time_step = 0.35


def pull(stretch, axis):
    squared = jnp.sum(stretch * stretch, axis=axis, keepdims=True)
    return stretch * (1.0 + 0.5 * squared / (1.0 + squared))


def lanes(offset):
    expanded = jnp.repeat(jnp.repeat(offset, BLOCK_ROWS, axis=-2), BLOCK_COLS, axis=-1)
    column = lax.broadcasted_iota(jnp.int32, expanded.shape, expanded.ndim - 1)
    block_start = column - column % BLOCK_COLS
    return (block_start + (column - block_start + expanded) % BLOCK_COLS).astype(jnp.int32)


def moved(field, lane_index):
    full_index = jnp.broadcast_to(lane_index[None], field.shape)
    return jnp.take_along_axis(field, full_index, axis=2)


def reference(positions, velocity, spring_class, match_shift, fixed, class_stiffness, cross_stiffness):
    padded_shift = jnp.pad(match_shift, ((2, 0), (0, 0), (0, 0), (0, 0)))
    moving = (fixed == 0).astype(jnp.float32)[:, None, None, None]

    def forces(current):
        padded = jnp.pad(current, ((2, 2), (0, 0), (0, 0), (0, 0)))

        def section_force(index_sec):
            nearby = lax.dynamic_slice_in_dim(padded, index_sec, 5, 0)
            shifts = lax.dynamic_slice_in_dim(padded_shift, index_sec, 3, 0)
            stiffness = class_stiffness[spring_class[index_sec]]
            center = nearby[2]
            across = center[:, :, 1:] - center[:, :, :-1]
            flow_across = stiffness[0][None, :, :-1] * pull(across, 0)
            summed = jnp.pad(flow_across, ((0, 0), (0, 0), (0, 1))) - jnp.pad(flow_across, ((0, 0), (0, 0), (1, 0)))
            down = center[:, 1:] - center[:, :-1]
            flow_down = stiffness[1][None, :-1] * pull(down, 0)
            summed = summed + jnp.pad(flow_down, ((0, 0), (0, 1), (0, 0))) - jnp.pad(flow_down, ((0, 0), (1, 0), (0, 0)))
            for hops in (1, 2):
                valid = (index_sec + hops < SECTIONS).astype(jnp.float32)
                partner = moved(nearby[2 + hops], lanes(shifts[2, hops - 1]))
                summed = summed + cross_stiffness[hops - 1] * pull(partner - center, 0) * valid
                before = (index_sec - hops >= 0).astype(jnp.float32)
                owner_shift = shifts[2 - hops, hops - 1]
                source = nearby[2 - hops]
                pair_term = cross_stiffness[hops - 1] * pull(moved(center, lanes(owner_shift)) - source, 0) * before
                summed = summed - moved(pair_term, lanes(-owner_shift))
            return summed

        return lax.map(section_force, jnp.arange(SECTIONS, dtype=jnp.int32))

    current = positions
    speed = velocity
    for step in range(STEPS):
        force = forces(current)
        speed = (damping_rate * speed + time_step * force) * moving
        current = current + time_step * speed
    return current, speed
```

```python
import functools

import jax
import jax.numpy as jnp
from jax import lax
from jax.experimental import pallas as pl
from jax.experimental.pallas import tpu as pltpu
from jax.sharding import PartitionSpec as P

BLOCK_ROWS = 8
LANES = 128
CLASSES = 8
DAMPING = 0.9
TIME_STEP = 0.35
ORDER = (1, 2, 0, 3)
HALO = 8


def pulled(ex, ey, k):
    r = 1.0 / (1.0 + (ex * ex + ey * ey))
    g = k * (1.5 - 0.5 * r)
    return ex * g, ey * g


def kernel(
    u_hbm, w_hbm, c_hbm, s_hbm, fixed, class_k, cross_k, ou_hbm, ow_hbm,
    ub, wb, cb, kh, kv, nxt, prv, ou, ow,
    edge_dn, edge_up, edge_top, edge_bot, shv, shp, sho,
    local_sem, out_sem, dn_send, dn_recv, up_send, up_recv,
    edn_send, edn_recv, eup_send, eup_recv, sh_send, sh_recv,
):
    n_sec, n_strip = lax.axis_size("sec"), lax.axis_size("strip")
    sec, strip = lax.axis_index("sec"), lax.axis_index("strip")
    has_prev, has_next = sec > 0, sec < n_sec - 1
    has_up, has_dn = strip > 0, strip < n_strip - 1
    prev_dev, next_dev = {"sec": sec - 1}, {"sec": sec + 1}
    up_dev, dn_dev = {"strip": strip - 1}, {"strip": strip + 1}
    sections, _, rows, width = u_hbm.shape
    blocks, tiles = rows // BLOCK_ROWS, width // LANES

    def remote(src, dst, send, recv, device):
        return pltpu.make_async_remote_copy(
            src_ref=src, dst_ref=dst, send_sem=send, recv_sem=recv,
            device_id=device, device_id_type=pl.DeviceIdType.MESH,
        )

    own = pl.ds(HALO, rows)
    loads = [
        pltpu.make_async_copy(u_hbm, ub.at[0, :, :, own, :], local_sem.at[0]),
        pltpu.make_async_copy(c_hbm, cb, local_sem.at[1]),
        pltpu.make_async_copy(w_hbm, wb, local_sem.at[2]),
        pltpu.make_async_copy(s_hbm, sho, local_sem.at[3]),
    ]
    for load in loads:
        load.start()

    barrier = pltpu.get_barrier_semaphore()
    near = ((has_prev, prev_dev), (has_next, next_dev), (has_up, up_dev), (has_dn, dn_dev))
    count = jnp.int32(0)
    for exists, device in near:
        count = count + exists.astype(jnp.int32)

        @pl.when(exists)
        def _():
            pl.semaphore_signal(
                barrier, inc=1, device_id=device, device_id_type=pl.DeviceIdType.MESH
            )
    pl.semaphore_wait(barrier, count)

    def to_prev(step, i):
        if step == 0:
            src = u_hbm.at[0:2, :, pl.ds(8 * i, 8), :]
        else:
            src = ub.at[1, 0:2, :, pl.ds(HALO + 8 * i, 8), :]
        return remote(src, nxt.at[step, :, :, pl.ds(8 * i, 8), :],
                      dn_send.at[step, i], dn_recv.at[step, i], prev_dev)

    def to_next(step, i):
        if step == 0:
            src = u_hbm.at[1:3, :, pl.ds(8 * i, 8), :]
        else:
            src = ub.at[1, 1:3, :, pl.ds(HALO + 8 * i, 8), :]
        return remote(src, prv.at[step, :, :, pl.ds(8 * i, 8), :],
                      up_send.at[step, i], up_recv.at[step, i], next_dev)

    def send_chunk(step, i):
        @pl.when(has_prev)
        def _():
            to_prev(step, i).start()

        @pl.when(has_next)
        def _():
            to_next(step, i).start()

    def edge_to_dn(step):
        used = pl.ds(0, (3 if step == 0 else 2) * sections)
        return remote(edge_dn.at[step, used], edge_top.at[step, used], edn_send.at[step], edn_recv.at[step], dn_dev)

    def edge_to_up(step):
        return remote(edge_up.at[step], edge_bot.at[step], eup_send.at[step], eup_recv.at[step], up_dev)

    shifts_to_next = remote(s_hbm.at[1:3], shv, sh_send, sh_recv, next_dev)

    @pl.when(has_next)
    def _():
        shifts_to_next.start()

    send_chunk(0, ORDER[0])
    send_chunk(0, ORDER[1])

    @pl.when(jnp.logical_not(has_prev))
    def _():
        prv[...] = jnp.zeros_like(prv)
        for a in range(2):
            for h in range(2):
                for i in range(blocks):
                    for j in range(tiles):
                        shp[a, h, i, j] = 0

    @pl.when(jnp.logical_not(has_next))
    def _():
        nxt[...] = jnp.zeros_like(nxt)

    @pl.when(jnp.logical_not(has_up))
    def _():
        edge_top[...] = jnp.zeros_like(edge_top)

    @pl.when(jnp.logical_not(has_dn))
    def _():
        edge_bot[...] = jnp.zeros_like(edge_bot)

    loads[1].wait()
    lane = lax.broadcasted_iota(jnp.int32, (BLOCK_ROWS, LANES), 1)
    row = lax.broadcasted_iota(jnp.int32, (BLOCK_ROWS, LANES), 0)
    table = [class_k[n] for n in range(CLASSES)]

    def stiffness(klass):
        out = jnp.full(klass.shape, table[0], jnp.float32)
        for n in range(1, CLASSES):
            out = jnp.where(klass == n, table[n], out)
        return out

    @pl.loop(0, tiles)
    def _(j):
        cols = pl.ds(pl.multiple_of(j * LANES, LANES), LANES)
        inside = jnp.logical_or(lane < LANES - 1, j < tiles - 1)
        for s in range(sections):
            for i in range(blocks):
                kh[s, pl.ds(8 * i, 8), cols] = jnp.where(
                    inside, stiffness(cb[s, 0, pl.ds(8 * i, 8), cols]), 0.0
                )
                below = stiffness(cb[s, 1, pl.ds(8 * i, 8), cols])
                if i == blocks - 1:
                    keep = jnp.logical_or(row < BLOCK_ROWS - 1, has_dn)
                    below = jnp.where(keep, below, 0.0)
                kv[s, pl.ds(HALO + 8 * i, 8), cols] = below

    loads[0].wait()

    def pack(step):
        for s in range(sections):
            for j in range(tiles):
                cols = pl.ds(j * LANES, LANES)
                for c in range(2):
                    edge_dn[step, 2 * s + c, pl.ds(j, 1), :] = ub[step, s, c, pl.ds(HALO + rows - 1, 1), cols]
                    edge_up[step, 2 * s + c, pl.ds(j, 1), :] = ub[step, s, c, pl.ds(HALO, 1), cols]
                if step == 0:
                    edge_dn[step, 2 * sections + s, pl.ds(j, 1), :] = kv[s, pl.ds(HALO + rows - 1, 1), cols]

    def send_edges(step):
        @pl.when(has_dn)
        def _():
            edge_to_dn(step).start()

        @pl.when(has_up)
        def _():
            edge_to_up(step).start()

    def unpack(step):
        @pl.when(has_up)
        def _():
            edge_to_dn(step).wait_recv()

        @pl.when(has_dn)
        def _():
            edge_to_up(step).wait_recv()

        for s in range(sections):
            for j in range(tiles):
                cols = pl.ds(j * LANES, LANES)
                for c in range(2):
                    ub[step, s, c, pl.ds(HALO - 1, 1), cols] = edge_top[step, 2 * s + c, pl.ds(j, 1), :]
                    ub[step, s, c, pl.ds(HALO + rows, 1), cols] = edge_bot[step, 2 * s + c, pl.ds(j, 1), :]
                if step == 0:
                    kv[s, pl.ds(HALO - 1, 1), cols] = edge_top[step, 2 * sections + s, pl.ds(j, 1), :]

    pack(0)
    send_edges(0)
    send_chunk(0, ORDER[2])
    send_chunk(0, ORDER[3])

    loads[2].wait()
    loads[3].wait()

    @pl.when(has_prev)
    def _():
        shifts_to_next.wait_recv()
        fetch = pltpu.make_async_copy(shv, shp, local_sem.at[4])
        fetch.start()
        fetch.wait()

    k1, k2 = cross_k[0], cross_k[1]
    zero = jnp.float32(0.0)
    k1n, k2n = jnp.where(has_next, k1, zero), jnp.where(has_next, k2, zero)
    k1p, k2p = jnp.where(has_prev, k1, zero), jnp.where(has_prev, k2, zero)
    moving = [jnp.where(fixed[s] == 0, jnp.float32(1.0), zero) for s in range(sections)]

    def ahead(pair, o):
        return [pltpu.roll(x, (-o) & (LANES - 1), 1) for x in pair]

    def behind(pair, o):
        return [pltpu.roll(x, o & (LANES - 1), 1) for x in pair]

    def update(step, i):
        here = pl.ds(8 * i, 8)
        mine = pl.ds(HALO + 8 * i, 8)
        above = pl.ds(HALO + 8 * i - 1, 8)
        below = pl.ds(HALO + 8 * i + 1, 8)

        def tile(j, carry):
            cols = pl.ds(pl.multiple_of(j * LANES, LANES), LANES)
            j_right = jnp.minimum(j + 1, tiles - 1)
            right_cols = pl.ds(pl.multiple_of(j_right * LANES, LANES), LANES)
            ahead_left, flow_left = carry
            u = [[ub[step, s, c, mine, cols] for c in range(2)] for s in range(sections)]
            force = [[None, None] for _ in range(sections)]
            new_ahead, new_flow = [], []

            def add(s, f):
                for c in range(2):
                    force[s][c] = f[c] if force[s][c] is None else force[s][c] + f[c]

            def sub(s, f):
                for c in range(2):
                    force[s][c] = force[s][c] - f[c]

            for s in range(sections):
                e = []
                for c in range(2):
                    coming = pltpu.roll(ub[step, s, c, mine, right_cols], LANES - 1, 1)
                    new_ahead.append(coming)
                    e.append(jnp.where(lane == LANES - 1, coming, ahead_left[2 * s + c]) - u[s][c])
                f = pulled(e[0], e[1], kh[s, here, cols])
                add(s, f)
                back = []
                for c in range(2):
                    turned = pltpu.roll(f[c], 1, 1)
                    new_flow.append(turned)
                    back.append(jnp.where(lane == 0, flow_left[2 * s + c], turned))
                sub(s, back)
                e = [ub[step, s, c, below, cols] - u[s][c] for c in range(2)]
                add(s, pulled(e[0], e[1], kv[s, mine, cols]))
                e = [u[s][c] - ub[step, s, c, above, cols] for c in range(2)]
                sub(s, pulled(e[0], e[1], kv[s, above, cols]))

            for s, h, k in ((0, 1, k1), (1, 1, k1), (0, 2, k2)):
                o = sho[s, h - 1, i, j]
                there = ahead(u[s + h], o)
                f = pulled(there[0] - u[s][0], there[1] - u[s][1], k)
                add(s, f)
                sub(s + h, behind(f, o))
            after = [[nxt[step, s, c, here, cols] for c in range(2)] for s in range(2)]
            for s, h, t, k in ((2, 1, 0, k1n), (1, 2, 0, k2n), (2, 2, 1, k2n)):
                there = ahead(after[t], sho[s, h - 1, i, j])
                add(s, pulled(there[0] - u[s][0], there[1] - u[s][1], k))
            before = [[prv[step, s, c, here, cols] for c in range(2)] for s in range(2)]
            for t, h, s, k in ((1, 1, 0, k1p), (0, 2, 0, k2p), (1, 2, 1, k2p)):
                there = behind(before[t], shp[t, h - 1, i, j])
                sub(s, pulled(u[s][0] - there[0], u[s][1] - there[1], k))

            for s in range(sections):
                for c in range(2):
                    speed = (DAMPING * wb[s, c, here, cols] + TIME_STEP * force[s][c]) * moving[s]
                    moved = u[s][c] + TIME_STEP * speed
                    if step == 0:
                        wb[s, c, here, cols] = speed
                        ub[1, s, c, mine, cols] = moved
                    else:
                        ow[s, c, here, cols] = speed
                        ou[s, c, here, cols] = moved
            return tuple(new_ahead), tuple(new_flow)

        first_cols = pl.ds(0, LANES)
        start = (
            tuple(
                pltpu.roll(ub[step, s, c, mine, first_cols], LANES - 1, 1)
                for s in range(sections)
                for c in range(2)
            ),
            tuple(jnp.zeros((BLOCK_ROWS, LANES), jnp.float32) for _ in range(2 * sections)),
        )
        lax.fori_loop(0, tiles, tile, start)

    def wait_chunk(step, i):
        @pl.when(has_next)
        def _():
            to_prev(step, i).wait_recv()

        @pl.when(has_prev)
        def _():
            to_next(step, i).wait_recv()

    outs = []
    for step in range(2):
        for n, i in enumerate(ORDER):
            if n == 2:
                unpack(step)
            wait_chunk(step, i)
            update(step, i)
            if step == 0:
                send_chunk(1, i)
                if n == 3:
                    pack(1)
                    send_edges(1)
            else:
                here = pl.ds(8 * i, 8)
                for k, (src, dst) in enumerate(((ou, ou_hbm), (ow, ow_hbm))):
                    copy = pltpu.make_async_copy(
                        src.at[:, :, here, :], dst.at[:, :, here, :], out_sem.at[k, i]
                    )
                    copy.start()
                    outs.append(copy)

    for step in range(2):
        for i in range(blocks):
            @pl.when(has_prev)
            def _():
                to_prev(step, i).wait_send()

            @pl.when(has_next)
            def _():
                to_next(step, i).wait_send()

        @pl.when(has_dn)
        def _():
            edge_to_dn(step).wait_send()

        @pl.when(has_up)
        def _():
            edge_to_up(step).wait_send()

    @pl.when(has_next)
    def _():
        shifts_to_next.wait_send()

    for copy in outs:
        copy.wait()


def per_device(positions, velocity, spring_class, match_shift, fixed, class_stiffness, cross_stiffness):
    sections, comps, rows, width = positions.shape
    blocks, tiles = rows // BLOCK_ROWS, width // LANES
    full = (sections, comps, rows, width)
    padded = rows + 2 * HALO
    f32, i32 = jnp.float32, jnp.int32
    any_spec = pl.BlockSpec(memory_space=pl.ANY)
    smem_spec = pl.BlockSpec(memory_space=pltpu.SMEM)
    dma = pltpu.SemaphoreType.DMA
    return pl.pallas_call(
        kernel,
        out_shape=(jax.ShapeDtypeStruct(full, f32), jax.ShapeDtypeStruct(full, f32)),
        in_specs=[any_spec] * 4 + [smem_spec] * 3,
        out_specs=(any_spec, any_spec),
        scratch_shapes=[
            pltpu.VMEM((2, sections, comps, padded, width), f32),
            pltpu.VMEM(full, f32),
            pltpu.VMEM(full, i32),
            pltpu.VMEM((sections, rows, width), f32),
            pltpu.VMEM((sections, padded, width), f32),
            pltpu.VMEM((2, 2, comps, rows, width), f32),
            pltpu.VMEM((2, 2, comps, rows, width), f32),
            pltpu.VMEM(full, f32),
            pltpu.VMEM(full, f32),
            pltpu.VMEM((2, 3 * sections, tiles, LANES), f32),
            pltpu.VMEM((2, 2 * sections, tiles, LANES), f32),
            pltpu.VMEM((2, 3 * sections, tiles, LANES), f32),
            pltpu.VMEM((2, 2 * sections, tiles, LANES), f32),
            pltpu.VMEM((2, 2, blocks, tiles), i32),
            pltpu.SMEM((2, 2, blocks, tiles), i32),
            pltpu.SMEM((sections, 2, blocks, tiles), i32),
            dma((5,)), dma((2, blocks)),
            dma((2, blocks)), dma((2, blocks)), dma((2, blocks)), dma((2, blocks)),
            dma((2,)), dma((2,)), dma((2,)), dma((2,)), dma(()), dma(()),
        ],
        compiler_params=pltpu.CompilerParams(collective_id=0, has_side_effects=True),
    )(positions, velocity, spring_class, match_shift, fixed, class_stiffness, cross_stiffness)


def solution(mesh):
    grid = P("sec", None, "strip", None)
    return jax.shard_map(
        per_device,
        mesh=mesh,
        in_specs=(grid, grid, grid, grid, P("sec"), P(), P()),
        out_specs=(grid, grid),
        check_vma=False,
    )
```

```python
import jax
import jax.numpy as jnp
from jax import lax
from jax.experimental import pallas as pl
from jax.experimental.pallas import tpu as pltpu
from jax.sharding import PartitionSpec as P

BLOCK_ROWS = 8
LANES = 128
CLASSES = 8
DAMPING = 0.9
TIME_STEP = 0.35
ORDER = (0, 3, 1, 2)


def pulled(ex, ey, k):
    r = 1.0 / (1.0 + (ex * ex + ey * ey))
    g = k * (1.5 - 0.5 * r)
    return ex * g, ey * g


def kernel(
    u_hbm, w_hbm, c_hbm, s_hbm, fixed, class_k, cross_k, ou, ow,
    ub, wb, cb, kh, kv, pf, nxt, prv,
    edge_dn, edge_up, edge_top, edge_bot, edge_class, edge_flow, shv, shp, sho,
    local_sem, dn_send, dn_recv, up_send, up_recv,
    edn_send, edn_recv, eup_send, eup_recv, sh_send, sh_recv,
):
    n_sec, n_strip = lax.axis_size("sec"), lax.axis_size("strip")
    sec, strip = lax.axis_index("sec"), lax.axis_index("strip")
    has_prev, has_next = sec > 0, sec < n_sec - 1
    has_up, has_dn = strip > 0, strip < n_strip - 1
    prev_dev, next_dev = {"sec": sec - 1}, {"sec": sec + 1}
    up_dev, dn_dev = {"strip": strip - 1}, {"strip": strip + 1}
    sections, _, rows, width = u_hbm.shape
    blocks, tiles = rows // BLOCK_ROWS, width // LANES
    lane = lax.broadcasted_iota(jnp.int32, (BLOCK_ROWS, LANES), 1)
    row = lax.broadcasted_iota(jnp.int32, (BLOCK_ROWS, LANES), 0)
    zero = jnp.float32(0.0)

    def rows_of(i):
        return pl.ds(BLOCK_ROWS * i, BLOCK_ROWS)

    def cols_of(j):
        return pl.ds(pl.multiple_of(j * LANES, LANES), LANES)

    def remote(src, dst, send, recv, device):
        return pltpu.make_async_remote_copy(
            src_ref=src, dst_ref=dst, send_sem=send, recv_sem=recv,
            device_id=device, device_id_type=pl.DeviceIdType.MESH,
        )

    barrier = pltpu.get_barrier_semaphore()
    near = ((has_prev, prev_dev), (has_next, next_dev), (has_up, up_dev), (has_dn, dn_dev))
    count = jnp.int32(0)
    for exists, device in near:
        count = count + exists.astype(jnp.int32)

        @pl.when(exists)
        def _():
            pl.semaphore_signal(
                barrier, inc=1, device_id=device, device_id_type=pl.DeviceIdType.MESH
            )

    loads = [
        pltpu.make_async_copy(u_hbm, ub.at[0], local_sem.at[0]),
        pltpu.make_async_copy(c_hbm, cb, local_sem.at[1]),
        pltpu.make_async_copy(s_hbm, sho, local_sem.at[2]),
        pltpu.make_async_copy(w_hbm, wb, local_sem.at[3]),
    ]
    for load in loads:
        load.start()

    def to_prev(step, i):
        src = u_hbm if step == 0 else ub.at[1]
        return remote(src.at[0:2, :, rows_of(i), :], nxt.at[step, :, :, rows_of(i), :],
                      dn_send.at[step, i], dn_recv.at[step, i], prev_dev)

    def to_next(step, i):
        src = u_hbm if step == 0 else ub.at[1]
        return remote(src.at[1:3, :, rows_of(i), :], prv.at[step, :, :, rows_of(i), :],
                      up_send.at[step, i], up_recv.at[step, i], next_dev)

    def send_chunk(step, i):
        @pl.when(has_prev)
        def _():
            to_prev(step, i).start()

        @pl.when(has_next)
        def _():
            to_next(step, i).start()

    def wait_chunk(step, i):
        @pl.when(has_next)
        def _():
            to_prev(step, i).wait_recv()

        @pl.when(has_prev)
        def _():
            to_next(step, i).wait_recv()

    def edge_to_dn(step):
        used = pl.ds(0, (3 if step == 0 else 2) * sections)
        return remote(edge_dn.at[step, used], edge_top.at[step, used],
                      edn_send.at[step], edn_recv.at[step], dn_dev)

    def edge_to_up(step):
        return remote(edge_up.at[step], edge_bot.at[step],
                      eup_send.at[step], eup_recv.at[step], up_dev)

    shifts_to_next = remote(s_hbm.at[1:3], shv, sh_send, sh_recv, next_dev)
    table = [class_k[n] for n in range(CLASSES)]

    def stiffness(klass):
        out = jnp.full(klass.shape, table[0], jnp.float32)
        for n in range(1, CLASSES):
            out = jnp.where(klass == n, table[n], out)
        return out

    def pack(step, last):
        dst, r = (edge_dn, rows - 1) if last else (edge_up, 0)
        for s in range(sections):
            for j in range(tiles):
                for c in range(2):
                    dst[step, 2 * s + c, pl.ds(j, 1), :] = ub[step, s, c, pl.ds(r, 1), pl.ds(j * LANES, LANES)]

    def send_edge(step, last):
        if last:
            @pl.when(has_dn)
            def _():
                edge_to_dn(step).start()
        else:
            @pl.when(has_up)
            def _():
                edge_to_up(step).start()

    loads[0].wait()
    pack(0, True)
    pack(0, False)
    loads[1].wait()
    for s in range(sections):
        for j in range(tiles):
            edge_class[s, pl.ds(j, 1), :] = cb[s, 1, pl.ds(rows - 1, 1), pl.ds(j * LANES, LANES)]
    for s in range(sections):
        edge_dn[0, 2 * sections + s] = stiffness(edge_class[s])

    pl.semaphore_wait(barrier, count)

    send_edge(0, True)
    send_edge(0, False)

    @pl.when(has_next)
    def _():
        shifts_to_next.start()

    for i in ORDER:
        send_chunk(0, i)

    @pl.when(jnp.logical_not(has_prev))
    def _():
        prv[...] = jnp.zeros_like(prv)
        for a in range(2):
            for h in range(2):
                for i in range(blocks):
                    for j in range(tiles):
                        shp[a, h, i, j] = 0

    @pl.when(jnp.logical_not(has_next))
    def _():
        nxt[...] = jnp.zeros_like(nxt)

    @pl.when(jnp.logical_not(has_up))
    def _():
        edge_top[...] = jnp.zeros_like(edge_top)

    @pl.when(jnp.logical_not(has_dn))
    def _():
        edge_bot[...] = jnp.zeros_like(edge_bot)

    def vertical(step):
        @pl.loop(0, tiles)
        def _(j):
            cols = cols_of(j)
            inside = jnp.logical_or(lane < LANES - 1, j < tiles - 1)
            for s in range(sections):
                u = [[ub[step, s, c, rows_of(i), cols] for c in range(2)] for i in range(blocks)]
                turned = [[pltpu.roll(x, BLOCK_ROWS - 1, 0) for x in pair] for pair in u]
                from_above = None
                for i in range(blocks):
                    if step == 0:
                        kh[s, rows_of(i), cols] = jnp.where(inside, stiffness(cb[s, 0, rows_of(i), cols]), 0.0)
                        k = stiffness(cb[s, 1, rows_of(i), cols])
                        if i == blocks - 1:
                            k = jnp.where(row < BLOCK_ROWS - 1, k, 0.0)
                        kv[s, rows_of(i), cols] = k
                    else:
                        k = kv[s, rows_of(i), cols]
                    e = []
                    for c in range(2):
                        below = turned[i][c]
                        if i < blocks - 1:
                            below = jnp.where(row == BLOCK_ROWS - 1, turned[i + 1][c], below)
                        e.append(below - u[i][c])
                    f = pulled(e[0], e[1], k)
                    down = [pltpu.roll(x, 1, 0) for x in f]
                    for c in range(2):
                        before = 0.0 if from_above is None else from_above[c]
                        pf[s, c, rows_of(i), cols] = f[c] - jnp.where(row == 0, before, down[c])
                    from_above = down

    def ahead(pair, o):
        return [pltpu.roll(x, (-o) & (LANES - 1), 1) for x in pair]

    def behind(pair, o):
        return [pltpu.roll(x, o & (LANES - 1), 1) for x in pair]

    def inner(step, i):
        here = rows_of(i)

        def tile(j, carry):
            cols, right_cols = cols_of(j), cols_of(jnp.minimum(j + 1, tiles - 1))
            ahead_left, flow_left = carry
            u = [[ub[step, s, c, here, cols] for c in range(2)] for s in range(sections)]
            force = [[pf[s, c, here, cols] for c in range(2)] for s in range(sections)]
            new_ahead, new_flow = [], []
            for s in range(sections):
                e = []
                for c in range(2):
                    coming = pltpu.roll(ub[step, s, c, here, right_cols], LANES - 1, 1)
                    new_ahead.append(coming)
                    e.append(jnp.where(lane == LANES - 1, coming, ahead_left[2 * s + c]) - u[s][c])
                f = pulled(e[0], e[1], kh[s, here, cols])
                for c in range(2):
                    turned = pltpu.roll(f[c], 1, 1)
                    new_flow.append(turned)
                    force[s][c] += f[c] - jnp.where(lane == 0, flow_left[2 * s + c], turned)
            for s, h, k in ((0, 1, k1), (1, 1, k1), (0, 2, k2)):
                o = sho[s, h - 1, i, j]
                there = ahead(u[s + h], o)
                f = pulled(there[0] - u[s][0], there[1] - u[s][1], k)
                back = behind(f, o)
                for c in range(2):
                    force[s][c] += f[c]
                    force[s + h][c] -= back[c]
            for s in range(sections):
                for c in range(2):
                    pf[s, c, here, cols] = force[s][c]
            return tuple(new_ahead), tuple(new_flow)

        start = (
            tuple(
                pltpu.roll(ub[step, s, c, here, pl.ds(0, LANES)], LANES - 1, 1)
                for s in range(sections)
                for c in range(2)
            ),
            tuple(jnp.zeros((BLOCK_ROWS, LANES), jnp.float32) for _ in range(2 * sections)),
        )
        lax.fori_loop(0, tiles, tile, start)

    def edge(step, last):
        if last:
            @pl.when(has_dn)
            def _():
                edge_to_up(step).wait_recv()
        else:
            @pl.when(has_up)
            def _():
                edge_to_dn(step).wait_recv()
        mine, theirs = (edge_dn, edge_bot) if last else (edge_up, edge_top)
        for s in range(sections):
            k = jnp.where(has_dn, edge_dn[0, 2 * sections + s], zero) if last else edge_top[0, 2 * sections + s]
            e = [theirs[step, 2 * s + c] - mine[step, 2 * s + c] for c in range(2)]
            f = pulled(e[0], e[1], k)
            for c in range(2):
                edge_flow[2 * s + c] = f[c]

    def outer(step, i):
        here = rows_of(i)
        edge_row = {0: 0, blocks - 1: BLOCK_ROWS - 1}.get(i)

        def tile(j, carry):
            cols = cols_of(j)
            u = [[ub[step, s, c, here, cols] for c in range(2)] for s in range(sections)]
            force = [[pf[s, c, here, cols] for c in range(2)] for s in range(sections)]
            if edge_row is not None:
                for s in range(sections):
                    for c in range(2):
                        f = jnp.broadcast_to(edge_flow[2 * s + c, pl.ds(j, 1), :], (BLOCK_ROWS, LANES))
                        force[s][c] += jnp.where(row == edge_row, f, 0.0)
            after = [[nxt[step, s, c, here, cols] for c in range(2)] for s in range(2)]
            for s, h, t, k in ((2, 1, 0, k1n), (1, 2, 0, k2n), (2, 2, 1, k2n)):
                there = ahead(after[t], sho[s, h - 1, i, j])
                f = pulled(there[0] - u[s][0], there[1] - u[s][1], k)
                for c in range(2):
                    force[s][c] += f[c]
            before = [[prv[step, s, c, here, cols] for c in range(2)] for s in range(2)]
            for t, h, s, k in ((1, 1, 0, k1p), (0, 2, 0, k2p), (1, 2, 1, k2p)):
                there = behind(before[t], shp[t, h - 1, i, j])
                f = pulled(there[0] - u[s][0], there[1] - u[s][1], k)
                for c in range(2):
                    force[s][c] += f[c]
            for s in range(sections):
                for c in range(2):
                    speed = (DAMPING * wb[s, c, here, cols] + TIME_STEP * force[s][c]) * moving[s]
                    moved = u[s][c] + TIME_STEP * speed
                    if step == 0:
                        wb[s, c, here, cols] = speed
                        ub[1, s, c, here, cols] = moved
                    else:
                        ow[s, c, here, cols] = speed
                        ou[s, c, here, cols] = moved
            return carry

        lax.fori_loop(0, tiles, tile, 0)

    k1, k2 = cross_k[0], cross_k[1]
    k1n, k2n = jnp.where(has_next, k1, zero), jnp.where(has_next, k2, zero)
    k1p, k2p = jnp.where(has_prev, k1, zero), jnp.where(has_prev, k2, zero)
    moving = [jnp.where(fixed[s] == 0, jnp.float32(1.0), zero) for s in range(sections)]

    for step in range(2):
        vertical(step)
        if step == 0:
            loads[2].wait()
        for n, i in enumerate(ORDER):
            inner(step, i)
            if step == 0 and n == 0:
                loads[3].wait()

                @pl.when(has_prev)
                def _():
                    shifts_to_next.wait_recv()
                    fetch = pltpu.make_async_copy(shv, shp, local_sem.at[4])
                    fetch.start()
                    fetch.wait()

            if i in (0, blocks - 1):
                edge(step, i != 0)
            wait_chunk(step, i)
            outer(step, i)
            if step == 0:
                send_chunk(1, i)
                if i in (0, blocks - 1):
                    pack(1, i != 0)
                    send_edge(1, i != 0)

    for step in range(2):
        for i in range(blocks):
            @pl.when(has_prev)
            def _():
                to_prev(step, i).wait_send()

            @pl.when(has_next)
            def _():
                to_next(step, i).wait_send()

        @pl.when(has_dn)
        def _():
            edge_to_dn(step).wait_send()

        @pl.when(has_up)
        def _():
            edge_to_up(step).wait_send()

    @pl.when(has_next)
    def _():
        shifts_to_next.wait_send()


def store(ou, ow, pos, vel, sem):
    copies = []
    for k, (src, dst) in enumerate(((ou, pos), (ow, vel))):
        for s in range(src.shape[0]):
            copies.append(pltpu.make_async_copy(src.at[s], dst.at[s], sem.at[k, s]))
    for copy in copies:
        copy.start()
    for copy in copies:
        copy.wait()


def per_device(positions, velocity, spring_class, match_shift, fixed, class_stiffness, cross_stiffness):
    sections, comps, rows, width = positions.shape
    blocks, tiles = rows // BLOCK_ROWS, width // LANES
    full = (sections, comps, rows, width)
    f32, i32 = jnp.float32, jnp.int32
    any_spec = pl.BlockSpec(memory_space=pl.ANY)
    smem_spec = pl.BlockSpec(memory_space=pltpu.SMEM)
    vmem_spec = pl.BlockSpec(memory_space=pltpu.VMEM)
    dma = pltpu.SemaphoreType.DMA
    moved, speed = pl.pallas_call(
        kernel,
        out_shape=(pltpu.VMEM(full, f32), pltpu.VMEM(full, f32)),
        in_specs=[any_spec] * 4 + [smem_spec] * 3,
        out_specs=(vmem_spec, vmem_spec),
        scratch_shapes=[
            pltpu.VMEM((2,) + full, f32),
            pltpu.VMEM(full, f32),
            pltpu.VMEM(full, i32),
            pltpu.VMEM((sections, rows, width), f32),
            pltpu.VMEM((sections, rows, width), f32),
            pltpu.VMEM(full, f32),
            pltpu.VMEM((2, 2, comps, rows, width), f32),
            pltpu.VMEM((2, 2, comps, rows, width), f32),
            pltpu.VMEM((2, 3 * sections, tiles, LANES), f32),
            pltpu.VMEM((2, 2 * sections, tiles, LANES), f32),
            pltpu.VMEM((2, 3 * sections, tiles, LANES), f32),
            pltpu.VMEM((2, 2 * sections, tiles, LANES), f32),
            pltpu.VMEM((sections, tiles, LANES), i32),
            pltpu.VMEM((2 * sections, tiles, LANES), f32),
            pltpu.VMEM((2, 2, blocks, tiles), i32),
            pltpu.SMEM((2, 2, blocks, tiles), i32),
            pltpu.SMEM((sections, 2, blocks, tiles), i32),
            dma((5,)),
            dma((2, blocks)), dma((2, blocks)), dma((2, blocks)), dma((2, blocks)),
            dma((2,)), dma((2,)), dma((2,)), dma((2,)), dma(()), dma(()),
        ],
        compiler_params=pltpu.CompilerParams(collective_id=0, has_side_effects=True),
        name="relax",
    )(positions, velocity, spring_class, match_shift, fixed, class_stiffness, cross_stiffness)
    moved = pltpu.with_memory_space_constraint(moved, pltpu.VMEM)
    speed = pltpu.with_memory_space_constraint(speed, pltpu.VMEM)
    return pl.pallas_call(
        store,
        out_shape=(jax.ShapeDtypeStruct(full, f32), jax.ShapeDtypeStruct(full, f32)),
        in_specs=[vmem_spec] * 2,
        out_specs=(any_spec, any_spec),
        scratch_shapes=[dma((2, sections))],
        name="store",
    )(moved, speed)


def solution(mesh):
    grid = P("sec", None, "strip", None)
    return jax.shard_map(
        per_device,
        mesh=mesh,
        in_specs=(grid, grid, grid, grid, P("sec"), P(), P()),
        out_specs=(grid, grid),
        check_vma=False,
    )
```

```python
import jax
import jax.numpy as jnp
from jax import lax
from jax.experimental import pallas as pl
from jax.experimental.pallas import tpu as pltpu
from jax.sharding import PartitionSpec as P

BLOCK_ROWS = 8
LANES = 128
CLASSES = 8
DAMPING = 0.9
TIME_STEP = 0.35
ORDERS = ((1, 3, 0, 2), (1, 2, 3, 0))
UNROLL = 4


def pulled(ex, ey, k):
    r = 1.0 / (1.0 + (ex * ex + ey * ey))
    g = k * (1.5 - 0.5 * r)
    return ex * g, ey * g


def kernel(
    u_hbm, w_hbm, c_hbm, s_hbm, fixed, class_k, cross_k, ou, ow,
    ub, wb, cb, kh, kv, pf, nxt, prv,
    edge_dn, edge_up, edge_top, edge_bot, edge_class, edge_flow, shv, shp, sho,
    local_sem, dn_send, dn_recv, up_send, up_recv,
    edn_send, edn_recv, eup_send, eup_recv, sh_send, sh_recv,
):
    n_sec, n_strip = lax.axis_size("sec"), lax.axis_size("strip")
    sec, strip = lax.axis_index("sec"), lax.axis_index("strip")
    has_prev, has_next = sec > 0, sec < n_sec - 1
    has_up, has_dn = strip > 0, strip < n_strip - 1
    prev_dev, next_dev = {"sec": sec - 1}, {"sec": sec + 1}
    up_dev, dn_dev = {"strip": strip - 1}, {"strip": strip + 1}
    sections, _, rows, width = u_hbm.shape
    blocks, tiles = rows // BLOCK_ROWS, width // LANES
    lane = lax.broadcasted_iota(jnp.int32, (BLOCK_ROWS, LANES), 1)
    row = lax.broadcasted_iota(jnp.int32, (BLOCK_ROWS, LANES), 0)
    zero = jnp.float32(0.0)

    def rows_of(i):
        return pl.ds(BLOCK_ROWS * i, BLOCK_ROWS)

    def cols_of(j):
        return pl.ds(pl.multiple_of(j * LANES, LANES), LANES)

    def remote(src, dst, send, recv, device):
        return pltpu.make_async_remote_copy(
            src_ref=src, dst_ref=dst, send_sem=send, recv_sem=recv,
            device_id=device, device_id_type=pl.DeviceIdType.MESH,
        )

    barrier = pltpu.get_barrier_semaphore()
    phase = lax.rem(strip, 4)
    up_mutual, dn_mutual = jnp.logical_and(has_up, phase == 3), jnp.logical_and(has_dn, phase == 2)
    up_leads = jnp.logical_and(has_up, jnp.logical_or(phase == 1, phase == 2))
    dn_leads = jnp.logical_and(has_dn, phase == 3)
    up_follows = jnp.logical_and(has_up, phase == 0)
    dn_follows = jnp.logical_and(has_dn, phase < 2)

    def greet(exists, device):
        @pl.when(exists)
        def _():
            pl.semaphore_signal(
                barrier, inc=1, device_id=device, device_id_type=pl.DeviceIdType.MESH
            )

    def number(*conditions):
        return sum((x.astype(jnp.int32) for x in conditions), jnp.int32(0))

    greet(has_prev, prev_dev)
    greet(has_next, next_dev)
    greet(up_mutual, up_dev)
    greet(dn_mutual, dn_dev)

    loads = [
        pltpu.make_async_copy(u_hbm, ub.at[0], local_sem.at[0]),
        pltpu.make_async_copy(c_hbm, cb, local_sem.at[1]),
        pltpu.make_async_copy(s_hbm, sho, local_sem.at[2]),
        pltpu.make_async_copy(w_hbm, wb, local_sem.at[3]),
    ]
    for load in loads:
        load.start()

    def to_prev(step, i):
        src = u_hbm if step == 0 else ub.at[1]
        return remote(src.at[0:2, :, rows_of(i), :], nxt.at[step, :, :, rows_of(i), :],
                      dn_send.at[step, i], dn_recv.at[step, i], prev_dev)

    def to_next(step, i):
        src = u_hbm if step == 0 else ub.at[1]
        return remote(src.at[1:3, :, rows_of(i), :], prv.at[step, :, :, rows_of(i), :],
                      up_send.at[step, i], up_recv.at[step, i], next_dev)

    def send_chunk(step, i):
        @pl.when(has_prev)
        def _():
            to_prev(step, i).start()

        @pl.when(has_next)
        def _():
            to_next(step, i).start()

    def wait_chunk(step, i):
        @pl.when(has_next)
        def _():
            to_prev(step, i).wait_recv()

        @pl.when(has_prev)
        def _():
            to_next(step, i).wait_recv()

    def edge_to_dn(step):
        used = pl.ds(0, (3 if step == 0 else 2) * sections)
        return remote(edge_dn.at[step, used], edge_top.at[step, used],
                      edn_send.at[step], edn_recv.at[step], dn_dev)

    def edge_to_up(step):
        return remote(edge_up.at[step], edge_bot.at[step],
                      eup_send.at[step], eup_recv.at[step], up_dev)

    shifts_to_next = remote(s_hbm.at[1:3], shv, sh_send, sh_recv, next_dev)
    table = [class_k[n] for n in range(CLASSES)]

    def stiffness(klass):
        out = jnp.full(klass.shape, table[0], jnp.float32)
        for n in range(1, CLASSES):
            out = jnp.where(klass == n, table[n], out)
        return out

    def pack(step, last):
        dst, r = (edge_dn, rows - 1) if last else (edge_up, 0)
        for s in range(sections):
            for j in range(tiles):
                for c in range(2):
                    dst[step, 2 * s + c, pl.ds(j, 1), :] = ub[step, s, c, pl.ds(r, 1), pl.ds(j * LANES, LANES)]

    def send_edge(step, last, allowed):
        @pl.when(allowed)
        def _():
            (edge_to_dn if last else edge_to_up)(step).start()

    loads[0].wait()
    pack(0, True)
    pack(0, False)
    loads[1].wait()
    for s in range(sections):
        for j in range(tiles):
            edge_class[s, pl.ds(j, 1), :] = cb[s, 1, pl.ds(rows - 1, 1), pl.ds(j * LANES, LANES)]
    for s in range(sections):
        edge_dn[0, 2 * sections + s] = stiffness(edge_class[s])

    pl.semaphore_wait(barrier, number(has_prev, has_next, up_mutual, dn_mutual, up_leads, dn_leads))
    for follows, leads, device in ((up_follows, up_leads, up_dev), (dn_follows, dn_leads, dn_dev)):
        greet(jnp.logical_or(follows, leads), device)
    send_edge(0, True, jnp.logical_or(dn_mutual, dn_leads))
    send_edge(0, False, jnp.logical_or(up_mutual, up_leads))

    @pl.when(has_next)
    def _():
        shifts_to_next.start()

    for i in ORDERS[0][:3]:
        send_chunk(0, i)

    @pl.when(jnp.logical_not(has_prev))
    def _():
        prv[...] = jnp.zeros_like(prv)
        for a in range(2):
            for h in range(2):
                for i in range(blocks):
                    for j in range(tiles):
                        shp[a, h, i, j] = 0

    @pl.when(jnp.logical_not(has_next))
    def _():
        nxt[...] = jnp.zeros_like(nxt)

    @pl.when(jnp.logical_not(has_up))
    def _():
        edge_top[...] = jnp.zeros_like(edge_top)

    @pl.when(jnp.logical_not(has_dn))
    def _():
        edge_bot[...] = jnp.zeros_like(edge_bot)

    def vertical(step):
        @pl.loop(0, tiles)
        def _(j):
            cols = cols_of(j)
            inside = jnp.logical_or(lane < LANES - 1, j < tiles - 1)
            for s in range(sections):
                u = [[ub[step, s, c, rows_of(i), cols] for c in range(2)] for i in range(blocks)]
                turned = [[pltpu.roll(x, BLOCK_ROWS - 1, 0) for x in pair] for pair in u]
                from_above = None
                for i in range(blocks):
                    if step == 0:
                        kh[s, rows_of(i), cols] = jnp.where(inside, stiffness(cb[s, 0, rows_of(i), cols]), 0.0)
                        k = stiffness(cb[s, 1, rows_of(i), cols])
                        if i == blocks - 1:
                            k = jnp.where(row < BLOCK_ROWS - 1, k, 0.0)
                        kv[s, rows_of(i), cols] = k
                    else:
                        k = kv[s, rows_of(i), cols]
                    e = []
                    for c in range(2):
                        below = turned[i][c]
                        if i < blocks - 1:
                            below = jnp.where(row == BLOCK_ROWS - 1, turned[i + 1][c], below)
                        e.append(below - u[i][c])
                    f = pulled(e[0], e[1], k)
                    down = [pltpu.roll(x, 1, 0) for x in f]
                    for c in range(2):
                        before = 0.0 if from_above is None else from_above[c]
                        pf[s, c, rows_of(i), cols] = f[c] - jnp.where(row == 0, before, down[c])
                    from_above = down

    def ahead(pair, o):
        return [pltpu.roll(x, (-o) & (LANES - 1), 1) for x in pair]

    def behind(pair, o):
        return [pltpu.roll(x, o & (LANES - 1), 1) for x in pair]

    def inner(step, i):
        here = rows_of(i)

        def tile(j, carry):
            cols, right_cols = cols_of(j), cols_of(jnp.minimum(j + 1, tiles - 1))
            ahead_left, flow_left = carry
            u = [[ub[step, s, c, here, cols] for c in range(2)] for s in range(sections)]
            force = [[pf[s, c, here, cols] for c in range(2)] for s in range(sections)]
            new_ahead, new_flow = [], []
            for s in range(sections):
                e = []
                for c in range(2):
                    coming = pltpu.roll(ub[step, s, c, here, right_cols], LANES - 1, 1)
                    new_ahead.append(coming)
                    e.append(jnp.where(lane == LANES - 1, coming, ahead_left[2 * s + c]) - u[s][c])
                f = pulled(e[0], e[1], kh[s, here, cols])
                for c in range(2):
                    turned = pltpu.roll(f[c], 1, 1)
                    new_flow.append(turned)
                    force[s][c] += f[c] - jnp.where(lane == 0, flow_left[2 * s + c], turned)
            for s, h, k in ((0, 1, k1), (1, 1, k1), (0, 2, k2)):
                o = sho[s, h - 1, i, j]
                there = ahead(u[s + h], o)
                f = pulled(there[0] - u[s][0], there[1] - u[s][1], k)
                back = behind(f, o)
                for c in range(2):
                    force[s][c] += f[c]
                    force[s + h][c] -= back[c]
            for s in range(sections):
                for c in range(2):
                    pf[s, c, here, cols] = force[s][c]
            return tuple(new_ahead), tuple(new_flow)

        start = (
            tuple(
                pltpu.roll(ub[step, s, c, here, pl.ds(0, LANES)], LANES - 1, 1)
                for s in range(sections)
                for c in range(2)
            ),
            tuple(jnp.zeros((BLOCK_ROWS, LANES), jnp.float32) for _ in range(2 * sections)),
        )
        lax.fori_loop(0, tiles, tile, start, unroll=min(UNROLL, tiles))

    def edge(step, last):
        if last:
            @pl.when(has_dn)
            def _():
                edge_to_up(step).wait_recv()
        else:
            @pl.when(has_up)
            def _():
                edge_to_dn(step).wait_recv()
        mine, theirs = (edge_dn, edge_bot) if last else (edge_up, edge_top)
        for s in range(sections):
            k = jnp.where(has_dn, edge_dn[0, 2 * sections + s], zero) if last else edge_top[0, 2 * sections + s]
            e = [theirs[step, 2 * s + c] - mine[step, 2 * s + c] for c in range(2)]
            f = pulled(e[0], e[1], k)
            for c in range(2):
                edge_flow[2 * s + c] = f[c]

    def outer(step, i):
        here = rows_of(i)
        edge_row = {0: 0, blocks - 1: BLOCK_ROWS - 1}.get(i)

        def tile(j, carry):
            cols = cols_of(j)
            u = [[ub[step, s, c, here, cols] for c in range(2)] for s in range(sections)]
            force = [[pf[s, c, here, cols] for c in range(2)] for s in range(sections)]
            if edge_row is not None:
                for s in range(sections):
                    for c in range(2):
                        f = jnp.broadcast_to(edge_flow[2 * s + c, pl.ds(j, 1), :], (BLOCK_ROWS, LANES))
                        force[s][c] += jnp.where(row == edge_row, f, 0.0)
            after = [[nxt[step, s, c, here, cols] for c in range(2)] for s in range(2)]
            for s, h, t, k in ((2, 1, 0, k1n), (1, 2, 0, k2n), (2, 2, 1, k2n)):
                there = ahead(after[t], sho[s, h - 1, i, j])
                f = pulled(there[0] - u[s][0], there[1] - u[s][1], k)
                for c in range(2):
                    force[s][c] += f[c]
            before = [[prv[step, s, c, here, cols] for c in range(2)] for s in range(2)]
            for t, h, s, k in ((1, 1, 0, k1p), (0, 2, 0, k2p), (1, 2, 1, k2p)):
                there = behind(before[t], shp[t, h - 1, i, j])
                f = pulled(there[0] - u[s][0], there[1] - u[s][1], k)
                for c in range(2):
                    force[s][c] += f[c]
            for s in range(sections):
                for c in range(2):
                    speed = (DAMPING * wb[s, c, here, cols] + TIME_STEP * force[s][c]) * moving[s]
                    moved = u[s][c] + TIME_STEP * speed
                    if step == 0:
                        wb[s, c, here, cols] = speed
                        ub[1, s, c, here, cols] = moved
                    else:
                        ow[s, c, here, cols] = speed
                        ou[s, c, here, cols] = moved
            return carry

        lax.fori_loop(0, tiles, tile, 0, unroll=min(UNROLL, tiles))

    k1, k2 = cross_k[0], cross_k[1]
    k1n, k2n = jnp.where(has_next, k1, zero), jnp.where(has_next, k2, zero)
    k1p, k2p = jnp.where(has_prev, k1, zero), jnp.where(has_prev, k2, zero)
    moving = [jnp.where(fixed[s] == 0, jnp.float32(1.0), zero) for s in range(sections)]

    for step in range(2):
        vertical(step)
        if step == 0:
            loads[2].wait()
        for n, i in enumerate(ORDERS[step]):
            inner(step, i)
            if step == 0 and n == 0:
                loads[3].wait()

                @pl.when(has_prev)
                def _():
                    shifts_to_next.wait_recv()
                    fetch = pltpu.make_async_copy(shv, shp, local_sem.at[4])
                    fetch.start()
                    fetch.wait()

            if i in (0, blocks - 1):
                edge(step, i != 0)
            wait_chunk(step, i)
            outer(step, i)
            if step == 0:
                if n == 0:
                    @pl.when(jnp.logical_or(up_follows, dn_follows))
                    def _():
                        pl.semaphore_wait(barrier, number(up_follows, dn_follows))

                    send_edge(0, True, dn_follows)
                    send_edge(0, False, up_follows)
                    send_chunk(0, ORDERS[0][3])
                    send_chunk(1, i)
                elif n == blocks - 1:
                    for k in ORDERS[1][1:]:
                        send_chunk(1, k)
                if i in (0, blocks - 1):
                    pack(1, i != 0)
                    send_edge(1, i != 0, has_dn if i else has_up)

    for step in range(2):
        for i in range(blocks):
            @pl.when(has_prev)
            def _():
                to_prev(step, i).wait_send()

            @pl.when(has_next)
            def _():
                to_next(step, i).wait_send()

        @pl.when(has_dn)
        def _():
            edge_to_dn(step).wait_send()

        @pl.when(has_up)
        def _():
            edge_to_up(step).wait_send()

    @pl.when(has_next)
    def _():
        shifts_to_next.wait_send()


def store(ou, ow, pos, vel, sem):
    copies = []
    for k, (src, dst) in enumerate(((ou, pos), (ow, vel))):
        for s in range(src.shape[0]):
            copies.append(pltpu.make_async_copy(src.at[s], dst.at[s], sem.at[k, s]))
    for copy in copies:
        copy.start()
    for copy in copies:
        copy.wait()


def per_device(positions, velocity, spring_class, match_shift, fixed, class_stiffness, cross_stiffness):
    sections, comps, rows, width = positions.shape
    blocks, tiles = rows // BLOCK_ROWS, width // LANES
    full = (sections, comps, rows, width)
    f32, i32 = jnp.float32, jnp.int32
    any_spec = pl.BlockSpec(memory_space=pl.ANY)
    smem_spec = pl.BlockSpec(memory_space=pltpu.SMEM)
    vmem_spec = pl.BlockSpec(memory_space=pltpu.VMEM)
    dma = pltpu.SemaphoreType.DMA
    moved, speed = pl.pallas_call(
        kernel,
        out_shape=(pltpu.VMEM(full, f32), pltpu.VMEM(full, f32)),
        in_specs=[any_spec] * 4 + [smem_spec] * 3,
        out_specs=(vmem_spec, vmem_spec),
        scratch_shapes=[
            pltpu.VMEM((2,) + full, f32),
            pltpu.VMEM(full, f32),
            pltpu.VMEM(full, i32),
            pltpu.VMEM((sections, rows, width), f32),
            pltpu.VMEM((sections, rows, width), f32),
            pltpu.VMEM(full, f32),
            pltpu.VMEM((2, 2, comps, rows, width), f32),
            pltpu.VMEM((2, 2, comps, rows, width), f32),
            pltpu.VMEM((2, 3 * sections, tiles, LANES), f32),
            pltpu.VMEM((2, 2 * sections, tiles, LANES), f32),
            pltpu.VMEM((2, 3 * sections, tiles, LANES), f32),
            pltpu.VMEM((2, 2 * sections, tiles, LANES), f32),
            pltpu.VMEM((sections, tiles, LANES), i32),
            pltpu.VMEM((2 * sections, tiles, LANES), f32),
            pltpu.VMEM((2, 2, blocks, tiles), i32),
            pltpu.SMEM((2, 2, blocks, tiles), i32),
            pltpu.SMEM((sections, 2, blocks, tiles), i32),
            dma((5,)),
            dma((2, blocks)), dma((2, blocks)), dma((2, blocks)), dma((2, blocks)),
            dma((2,)), dma((2,)), dma((2,)), dma((2,)), dma(()), dma(()),
        ],
        compiler_params=pltpu.CompilerParams(collective_id=0, has_side_effects=True),
        name="relax",
    )(positions, velocity, spring_class, match_shift, fixed, class_stiffness, cross_stiffness)
    moved = pltpu.with_memory_space_constraint(moved, pltpu.VMEM)
    speed = pltpu.with_memory_space_constraint(speed, pltpu.VMEM)
    return pl.pallas_call(
        store,
        out_shape=(jax.ShapeDtypeStruct(full, f32), jax.ShapeDtypeStruct(full, f32)),
        in_specs=[vmem_spec] * 2,
        out_specs=(any_spec, any_spec),
        scratch_shapes=[dma((2, sections))],
        name="store",
    )(moved, speed)


def solution(mesh):
    grid = P("sec", None, "strip", None)
    return jax.shard_map(
        per_device,
        mesh=mesh,
        in_specs=(grid, grid, grid, grid, P("sec"), P(), P()),
        out_specs=(grid, grid),
        check_vma=False,
    )
```

```python
import jax
import jax.numpy as jnp
from jax import lax
from jax.experimental import pallas as pl
from jax.experimental.pallas import tpu as pltpu
from jax.sharding import PartitionSpec as P

BLOCK_ROWS = 8
LANES = 128
CLASSES = 8
DAMPING = 0.9
TIME_STEP = 0.35
ORDERS = ((1, 3, 0, 2), (1, 2, 3, 0))
RELAYED = ((2, 0, 3), (3, 1, 0))
GROUP = 4
UNROLL = 4


def pulled(ex, ey, k):
    r = 1.0 / (1.0 + (ex * ex + ey * ey))
    g = k * (1.5 - 0.5 * r)
    return ex * g, ey * g


def kernel(
    u_hbm, w_hbm, c_hbm, s_hbm, fixed, class_k, cross_k, ou, ow,
    ub, wb, cb, kh, kv, pf, nxt, prv, rel,
    edge_dn, edge_up, edge_top, edge_bot, edge_class, edge_flow, shv, shp, sho,
    local_sem, dn_send, dn_recv, up_send, up_recv,
    rel_send, rel_recv, edn_send, edn_recv, eup_send, eup_recv, sh_send, sh_recv,
):
    n_sec, n_strip = lax.axis_size("sec"), lax.axis_size("strip")
    sec, strip = lax.axis_index("sec"), lax.axis_index("strip")
    has_prev, has_next = sec > 0, sec < n_sec - 1
    has_up, has_dn = strip > 0, strip < n_strip - 1
    prev_dev, next_dev = {"sec": sec - 1}, {"sec": sec + 1}
    up_dev, dn_dev = {"strip": strip - 1}, {"strip": strip + 1}
    groups, group = n_sec // GROUP, sec // GROUP
    is_first = jnp.logical_and(lax.rem(sec, GROUP) == 0, group < groups)
    is_last = lax.rem(sec, GROUP) == GROUP - 1
    far_next, far_prev = sec + GROUP < groups * GROUP, sec >= GROUP
    via_up = jnp.where(jnp.logical_and(is_last, far_next), group + 1, 0)
    via_dn = jnp.where(jnp.logical_and(is_first, far_prev), groups - group, 0)
    relay_up, relay_dn = jnp.logical_and(is_last, far_prev), jnp.logical_and(is_first, far_next)
    relays = jnp.where(relay_up, group, jnp.where(relay_dn, groups - 1 - group, 0))
    sections, _, rows, width = u_hbm.shape
    blocks, tiles = rows // BLOCK_ROWS, width // LANES
    lane = lax.broadcasted_iota(jnp.int32, (BLOCK_ROWS, LANES), 1)
    row = lax.broadcasted_iota(jnp.int32, (BLOCK_ROWS, LANES), 0)
    zero = jnp.float32(0.0)

    def rows_of(i):
        return pl.ds(BLOCK_ROWS * i, BLOCK_ROWS)

    def cols_of(j):
        return pl.ds(pl.multiple_of(j * LANES, LANES), LANES)

    def remote(src, dst, send, recv, device):
        return pltpu.make_async_remote_copy(
            src_ref=src, dst_ref=dst, send_sem=send, recv_sem=recv,
            device_id=device, device_id_type=pl.DeviceIdType.MESH,
        )

    barrier = pltpu.get_barrier_semaphore()
    phase = lax.rem(strip, 4)
    up_mutual, dn_mutual = jnp.logical_and(has_up, phase == 3), jnp.logical_and(has_dn, phase == 2)
    up_leads = jnp.logical_and(has_up, jnp.logical_or(phase == 1, phase == 2))
    dn_leads = jnp.logical_and(has_dn, phase == 3)
    up_follows = jnp.logical_and(has_up, phase == 0)
    dn_follows = jnp.logical_and(has_dn, phase < 2)

    def greet(exists, device):
        @pl.when(exists)
        def _():
            pl.semaphore_signal(
                barrier, inc=1, device_id=device, device_id_type=pl.DeviceIdType.MESH
            )

    def number(*conditions):
        return sum((x.astype(jnp.int32) for x in conditions), jnp.int32(0))

    greet(has_prev, prev_dev)
    greet(has_next, next_dev)
    far = [
        (jnp.logical_and(jnp.logical_or(is_first, is_last), far_next), {"sec": sec + GROUP}),
        (jnp.logical_and(jnp.logical_or(is_first, is_last), far_prev), {"sec": sec - GROUP}),
    ]
    if groups > 1:
        far.append((is_first, {"sec": sec + GROUP - 1}))
        far.append((is_last, {"sec": sec - GROUP + 1}))
    for exists, device in far:
        greet(exists, device)
    greet(up_mutual, up_dev)
    greet(dn_mutual, dn_dev)

    loads = [
        pltpu.make_async_copy(u_hbm, ub.at[0], local_sem.at[0]),
        pltpu.make_async_copy(c_hbm, cb, local_sem.at[1]),
        pltpu.make_async_copy(s_hbm, sho, local_sem.at[2]),
        pltpu.make_async_copy(w_hbm, wb, local_sem.at[3]),
    ]
    for load in loads:
        load.start()

    def part(step, first, i):
        src = u_hbm if step == 0 else ub.at[1]
        return src.at[first:first + 2, :, rows_of(i), :]

    def to_prev(step, i):
        return remote(part(step, 0, i), nxt.at[step, :, :, rows_of(i), :],
                      dn_send.at[step, i], dn_recv.at[step, i], prev_dev)

    def to_next(step, i):
        return remote(part(step, 1, i), prv.at[step, :, :, rows_of(i), :],
                      up_send.at[step, i], up_recv.at[step, i], next_dev)

    def to_relay(step, i, up):
        return remote(part(step, 1 if up else 0, i), rel.at[step, i],
                      (up_send if up else dn_send).at[step, i], rel_recv.at[step, i],
                      {"sec": sec + GROUP if up else sec - GROUP})

    def from_relay(step, i, up):
        return remote(rel.at[step, i], (prv if up else nxt).at[step, :, :, rows_of(i), :],
                      rel_send.at[step, i], (up_recv if up else dn_recv).at[step, i],
                      {"sec": sec - GROUP + 1 if up else sec + GROUP - 1})

    def by_relay(step, i, count):
        return RELAYED[step].index(i) < count if i in RELAYED[step] else jnp.bool_(False)

    def send_chunk(step, i):
        @pl.when(jnp.logical_and(has_prev, jnp.logical_not(by_relay(step, i, via_dn))))
        def _():
            to_prev(step, i).start()

        @pl.when(jnp.logical_and(has_next, jnp.logical_not(by_relay(step, i, via_up))))
        def _():
            to_next(step, i).start()

    def send_by_relay(step, i):
        if i in RELAYED[step]:
            @pl.when(by_relay(step, i, via_dn))
            def _():
                to_relay(step, i, False).start()

            @pl.when(by_relay(step, i, via_up))
            def _():
                to_relay(step, i, True).start()

    def forward_first(n):
        for count in range(n + 1, len(RELAYED[0]) + 1):
            forward(0, RELAYED[0][count - 1 - n], relays == count)

    def forward(step, i, when=None):
        mine = by_relay(step, i, relays) if when is None else when

        @pl.when(mine)
        def _():
            to_relay(step, i, True).wait_recv()

        @pl.when(jnp.logical_and(mine, relay_up))
        def _():
            from_relay(step, i, True).start()

        @pl.when(jnp.logical_and(mine, relay_dn))
        def _():
            from_relay(step, i, False).start()

    def wait_chunk(step, i):
        @pl.when(has_next)
        def _():
            to_prev(step, i).wait_recv()

        @pl.when(has_prev)
        def _():
            to_next(step, i).wait_recv()

    def edge_to_dn(step):
        used = pl.ds(0, (3 if step == 0 else 2) * sections)
        return remote(edge_dn.at[step, used], edge_top.at[step, used],
                      edn_send.at[step], edn_recv.at[step], dn_dev)

    def edge_to_up(step):
        return remote(edge_up.at[step], edge_bot.at[step],
                      eup_send.at[step], eup_recv.at[step], up_dev)

    shifts_to_next = remote(s_hbm.at[1:3], shv, sh_send, sh_recv, next_dev)
    table = [class_k[n] for n in range(CLASSES)]

    def stiffness(klass):
        out = jnp.full(klass.shape, table[0], jnp.float32)
        for n in range(1, CLASSES):
            out = jnp.where(klass == n, table[n], out)
        return out

    def pack(step, last):
        dst, r = (edge_dn, rows - 1) if last else (edge_up, 0)
        for s in range(sections):
            for j in range(tiles):
                for c in range(2):
                    dst[step, 2 * s + c, pl.ds(j, 1), :] = ub[step, s, c, pl.ds(r, 1), pl.ds(j * LANES, LANES)]

    def send_edge(step, last, allowed):
        @pl.when(allowed)
        def _():
            (edge_to_dn if last else edge_to_up)(step).start()

    loads[0].wait()
    pack(0, True)
    pack(0, False)
    loads[1].wait()
    for s in range(sections):
        for j in range(tiles):
            edge_class[s, pl.ds(j, 1), :] = cb[s, 1, pl.ds(rows - 1, 1), pl.ds(j * LANES, LANES)]
    for s in range(sections):
        edge_dn[0, 2 * sections + s] = stiffness(edge_class[s])

    pl.semaphore_wait(
        barrier,
        number(has_prev, has_next, up_mutual, dn_mutual, up_leads, dn_leads, *(exists for exists, _ in far)),
    )
    for follows, leads, device in ((up_follows, up_leads, up_dev), (dn_follows, dn_leads, dn_dev)):
        greet(jnp.logical_or(follows, leads), device)
    send_edge(0, True, jnp.logical_or(dn_mutual, dn_leads))
    send_edge(0, False, jnp.logical_or(up_mutual, up_leads))

    @pl.when(has_next)
    def _():
        shifts_to_next.start()

    for i in ORDERS[0]:
        send_by_relay(0, i)
    for i in ORDERS[0][:3]:
        send_chunk(0, i)

    @pl.when(jnp.logical_not(has_prev))
    def _():
        prv[...] = jnp.zeros_like(prv)
        for a in range(2):
            for h in range(2):
                for i in range(blocks):
                    for j in range(tiles):
                        shp[a, h, i, j] = 0

    @pl.when(jnp.logical_not(has_next))
    def _():
        nxt[...] = jnp.zeros_like(nxt)

    @pl.when(jnp.logical_not(has_up))
    def _():
        edge_top[...] = jnp.zeros_like(edge_top)

    @pl.when(jnp.logical_not(has_dn))
    def _():
        edge_bot[...] = jnp.zeros_like(edge_bot)

    def vertical(step):
        @pl.loop(0, tiles)
        def _(j):
            cols = cols_of(j)
            inside = jnp.logical_or(lane < LANES - 1, j < tiles - 1)
            for s in range(sections):
                u = [[ub[step, s, c, rows_of(i), cols] for c in range(2)] for i in range(blocks)]
                turned = [[pltpu.roll(x, BLOCK_ROWS - 1, 0) for x in pair] for pair in u]
                from_above = None
                for i in range(blocks):
                    if step == 0:
                        kh[s, rows_of(i), cols] = jnp.where(inside, stiffness(cb[s, 0, rows_of(i), cols]), 0.0)
                        k = stiffness(cb[s, 1, rows_of(i), cols])
                        if i == blocks - 1:
                            k = jnp.where(row < BLOCK_ROWS - 1, k, 0.0)
                        kv[s, rows_of(i), cols] = k
                    else:
                        k = kv[s, rows_of(i), cols]
                    e = []
                    for c in range(2):
                        below = turned[i][c]
                        if i < blocks - 1:
                            below = jnp.where(row == BLOCK_ROWS - 1, turned[i + 1][c], below)
                        e.append(below - u[i][c])
                    f = pulled(e[0], e[1], k)
                    down = [pltpu.roll(x, 1, 0) for x in f]
                    for c in range(2):
                        before = 0.0 if from_above is None else from_above[c]
                        pf[s, c, rows_of(i), cols] = f[c] - jnp.where(row == 0, before, down[c])
                    from_above = down

    def ahead(pair, o):
        return [pltpu.roll(x, (-o) & (LANES - 1), 1) for x in pair]

    def behind(pair, o):
        return [pltpu.roll(x, o & (LANES - 1), 1) for x in pair]

    def inner(step, i):
        here = rows_of(i)

        def tile(j, carry):
            cols, right_cols = cols_of(j), cols_of(jnp.minimum(j + 1, tiles - 1))
            ahead_left, flow_left = carry
            u = [[ub[step, s, c, here, cols] for c in range(2)] for s in range(sections)]
            force = [[pf[s, c, here, cols] for c in range(2)] for s in range(sections)]
            new_ahead, new_flow = [], []
            for s in range(sections):
                e = []
                for c in range(2):
                    coming = pltpu.roll(ub[step, s, c, here, right_cols], LANES - 1, 1)
                    new_ahead.append(coming)
                    e.append(jnp.where(lane == LANES - 1, coming, ahead_left[2 * s + c]) - u[s][c])
                f = pulled(e[0], e[1], kh[s, here, cols])
                for c in range(2):
                    turned = pltpu.roll(f[c], 1, 1)
                    new_flow.append(turned)
                    force[s][c] += f[c] - jnp.where(lane == 0, flow_left[2 * s + c], turned)
            for s, h, k in ((0, 1, k1), (1, 1, k1), (0, 2, k2)):
                o = sho[s, h - 1, i, j]
                there = ahead(u[s + h], o)
                f = pulled(there[0] - u[s][0], there[1] - u[s][1], k)
                back = behind(f, o)
                for c in range(2):
                    force[s][c] += f[c]
                    force[s + h][c] -= back[c]
            for s in range(sections):
                for c in range(2):
                    pf[s, c, here, cols] = force[s][c]
            return tuple(new_ahead), tuple(new_flow)

        start = (
            tuple(
                pltpu.roll(ub[step, s, c, here, pl.ds(0, LANES)], LANES - 1, 1)
                for s in range(sections)
                for c in range(2)
            ),
            tuple(jnp.zeros((BLOCK_ROWS, LANES), jnp.float32) for _ in range(2 * sections)),
        )
        lax.fori_loop(0, tiles, tile, start, unroll=min(UNROLL, tiles))

    def edge(step, last):
        if last:
            @pl.when(has_dn)
            def _():
                edge_to_up(step).wait_recv()
        else:
            @pl.when(has_up)
            def _():
                edge_to_dn(step).wait_recv()
        mine, theirs = (edge_dn, edge_bot) if last else (edge_up, edge_top)
        for s in range(sections):
            k = jnp.where(has_dn, edge_dn[0, 2 * sections + s], zero) if last else edge_top[0, 2 * sections + s]
            e = [theirs[step, 2 * s + c] - mine[step, 2 * s + c] for c in range(2)]
            f = pulled(e[0], e[1], k)
            for c in range(2):
                edge_flow[2 * s + c] = f[c]

    def outer(step, i):
        here = rows_of(i)
        edge_row = {0: 0, blocks - 1: BLOCK_ROWS - 1}.get(i)

        def tile(j, carry):
            cols = cols_of(j)
            u = [[ub[step, s, c, here, cols] for c in range(2)] for s in range(sections)]
            force = [[pf[s, c, here, cols] for c in range(2)] for s in range(sections)]
            if edge_row is not None:
                for s in range(sections):
                    for c in range(2):
                        f = jnp.broadcast_to(edge_flow[2 * s + c, pl.ds(j, 1), :], (BLOCK_ROWS, LANES))
                        force[s][c] += jnp.where(row == edge_row, f, 0.0)
            after = [[nxt[step, s, c, here, cols] for c in range(2)] for s in range(2)]
            for s, h, t, k in ((2, 1, 0, k1n), (1, 2, 0, k2n), (2, 2, 1, k2n)):
                there = ahead(after[t], sho[s, h - 1, i, j])
                f = pulled(there[0] - u[s][0], there[1] - u[s][1], k)
                for c in range(2):
                    force[s][c] += f[c]
            before = [[prv[step, s, c, here, cols] for c in range(2)] for s in range(2)]
            for t, h, s, k in ((1, 1, 0, k1p), (0, 2, 0, k2p), (1, 2, 1, k2p)):
                there = behind(before[t], shp[t, h - 1, i, j])
                f = pulled(there[0] - u[s][0], there[1] - u[s][1], k)
                for c in range(2):
                    force[s][c] += f[c]
            for s in range(sections):
                for c in range(2):
                    speed = (DAMPING * wb[s, c, here, cols] + TIME_STEP * force[s][c]) * moving[s]
                    moved = u[s][c] + TIME_STEP * speed
                    if step == 0:
                        wb[s, c, here, cols] = speed
                        ub[1, s, c, here, cols] = moved
                    else:
                        ow[s, c, here, cols] = speed
                        ou[s, c, here, cols] = moved
            return carry

        lax.fori_loop(0, tiles, tile, 0, unroll=min(UNROLL, tiles))

    k1, k2 = cross_k[0], cross_k[1]
    k1n, k2n = jnp.where(has_next, k1, zero), jnp.where(has_next, k2, zero)
    k1p, k2p = jnp.where(has_prev, k1, zero), jnp.where(has_prev, k2, zero)
    moving = [jnp.where(fixed[s] == 0, jnp.float32(1.0), zero) for s in range(sections)]

    for step in range(2):
        vertical(step)
        if step == 0:
            loads[2].wait()
        for n, i in enumerate(ORDERS[step]):
            inner(step, i)
            if step == 0 and n == 0:
                loads[3].wait()

                @pl.when(has_prev)
                def _():
                    shifts_to_next.wait_recv()
                    fetch = pltpu.make_async_copy(shv, shp, local_sem.at[4])
                    fetch.start()
                    fetch.wait()

                forward_first(0)
            elif step == 0 and n == 1:
                forward_first(2)
            elif step == 0 and n == 3:
                forward(1, RELAYED[1][0])
            elif step == 1 and n == 0:
                forward(1, RELAYED[1][2])

            if i in (0, blocks - 1):
                edge(step, i != 0)
            wait_chunk(step, i)
            outer(step, i)
            if step == 0:
                send_by_relay(1, i)
                if n == 0:
                    forward_first(1)

                    @pl.when(jnp.logical_or(up_follows, dn_follows))
                    def _():
                        pl.semaphore_wait(barrier, number(up_follows, dn_follows))

                    send_edge(0, True, dn_follows)
                    send_edge(0, False, up_follows)
                if i in (0, blocks - 1):
                    pack(1, i != 0)
                    send_edge(1, i != 0, has_dn if i else has_up)
                if n == 1:
                    send_chunk(0, ORDERS[0][3])
                    send_chunk(1, ORDERS[1][0])
                elif n == 2:
                    forward(1, RELAYED[1][1])
                elif n == 3:
                    for k in ORDERS[1][1:]:
                        send_chunk(1, k)

    for step in range(2):
        for i in RELAYED[step]:
            @pl.when(by_relay(step, i, relays))
            def _():
                from_relay(step, i, True).wait_send()

        for i in range(blocks):
            @pl.when(has_prev)
            def _():
                to_prev(step, i).wait_send()

            @pl.when(has_next)
            def _():
                to_next(step, i).wait_send()

        @pl.when(has_dn)
        def _():
            edge_to_dn(step).wait_send()

        @pl.when(has_up)
        def _():
            edge_to_up(step).wait_send()

    @pl.when(has_next)
    def _():
        shifts_to_next.wait_send()


def store(ou, ow, pos, vel, sem):
    copies = []
    for k, (src, dst) in enumerate(((ou, pos), (ow, vel))):
        for s in range(src.shape[0]):
            copies.append(pltpu.make_async_copy(src.at[s], dst.at[s], sem.at[k, s]))
    for copy in copies:
        copy.start()
    for copy in copies:
        copy.wait()


def per_device(positions, velocity, spring_class, match_shift, fixed, class_stiffness, cross_stiffness):
    sections, comps, rows, width = positions.shape
    blocks, tiles = rows // BLOCK_ROWS, width // LANES
    full = (sections, comps, rows, width)
    f32, i32 = jnp.float32, jnp.int32
    any_spec = pl.BlockSpec(memory_space=pl.ANY)
    smem_spec = pl.BlockSpec(memory_space=pltpu.SMEM)
    vmem_spec = pl.BlockSpec(memory_space=pltpu.VMEM)
    dma = pltpu.SemaphoreType.DMA
    moved, speed = pl.pallas_call(
        kernel,
        out_shape=(pltpu.VMEM(full, f32), pltpu.VMEM(full, f32)),
        in_specs=[any_spec] * 4 + [smem_spec] * 3,
        out_specs=(vmem_spec, vmem_spec),
        scratch_shapes=[
            pltpu.VMEM((2,) + full, f32),
            pltpu.VMEM(full, f32),
            pltpu.VMEM(full, i32),
            pltpu.VMEM((sections, rows, width), f32),
            pltpu.VMEM((sections, rows, width), f32),
            pltpu.VMEM(full, f32),
            pltpu.VMEM((2, 2, comps, rows, width), f32),
            pltpu.VMEM((2, 2, comps, rows, width), f32),
            pltpu.VMEM((2, blocks, 2, comps, BLOCK_ROWS, width), f32),
            pltpu.VMEM((2, 3 * sections, tiles, LANES), f32),
            pltpu.VMEM((2, 2 * sections, tiles, LANES), f32),
            pltpu.VMEM((2, 3 * sections, tiles, LANES), f32),
            pltpu.VMEM((2, 2 * sections, tiles, LANES), f32),
            pltpu.VMEM((sections, tiles, LANES), i32),
            pltpu.VMEM((2 * sections, tiles, LANES), f32),
            pltpu.VMEM((2, 2, blocks, tiles), i32),
            pltpu.SMEM((2, 2, blocks, tiles), i32),
            pltpu.SMEM((sections, 2, blocks, tiles), i32),
            dma((5,)),
            dma((2, blocks)), dma((2, blocks)), dma((2, blocks)), dma((2, blocks)),
            dma((2, blocks)), dma((2, blocks)),
            dma((2,)), dma((2,)), dma((2,)), dma((2,)), dma(()), dma(()),
        ],
        compiler_params=pltpu.CompilerParams(collective_id=0, has_side_effects=True),
        name="relax",
    )(positions, velocity, spring_class, match_shift, fixed, class_stiffness, cross_stiffness)
    moved = pltpu.with_memory_space_constraint(moved, pltpu.VMEM)
    speed = pltpu.with_memory_space_constraint(speed, pltpu.VMEM)
    return pl.pallas_call(
        store,
        out_shape=(jax.ShapeDtypeStruct(full, f32), jax.ShapeDtypeStruct(full, f32)),
        in_specs=[vmem_spec] * 2,
        out_specs=(any_spec, any_spec),
        scratch_shapes=[dma((2, sections))],
        name="store",
    )(moved, speed)


def solution(mesh):
    grid = P("sec", None, "strip", None)
    return jax.shard_map(
        per_device,
        mesh=mesh,
        in_specs=(grid, grid, grid, grid, P("sec"), P(), P()),
        out_specs=(grid, grid),
        check_vma=False,
    )
```

```python
import jax
import jax.numpy as jnp
from jax import lax
from jax.experimental import pallas as pl
from jax.experimental.pallas import tpu as pltpu
from jax.sharding import PartitionSpec as P

BLOCK_ROWS = 8
LANES = 128
CLASSES = 8
DAMPING = 0.9
TIME_STEP = 0.35
ORDER = (1, 3, 0, 2)
RELAYED = ((2, 0, 3), (3, 1, 0))
GROUP = 4
UNROLL = 4


def pulled(ex, ey, k):
    r = 1.0 / (1.0 + (ex * ex + ey * ey))
    g = k * (1.5 - 0.5 * r)
    return ex * g, ey * g


def kernel(
    u_hbm, w_hbm, c_hbm, s_hbm, fixed_hbm, class_hbm, cross_hbm, ou, ow, fixed, class_k, cross_k,
    ub, wb, cb, kh, kv, pf, nxt, prv, rel,
    edge_dn, edge_up, edge_top, edge_bot, edge_class, edge_flow, shv, shp, sho,
    local_sem, dn_send, dn_recv, up_send, up_recv,
    rel_send, rel_recv, edn_send, edn_recv, eup_send, eup_recv, sh_send, sh_recv,
):
    n_sec, n_strip = lax.axis_size("sec"), lax.axis_size("strip")
    sec, strip = lax.axis_index("sec"), lax.axis_index("strip")
    has_prev, has_next = sec > 0, sec < n_sec - 1
    has_up, has_dn = strip > 0, strip < n_strip - 1
    prev_dev, next_dev = {"sec": sec - 1}, {"sec": sec + 1}
    up_dev, dn_dev = {"strip": strip - 1}, {"strip": strip + 1}
    groups, group = n_sec // GROUP, sec // GROUP
    is_first = jnp.logical_and(lax.rem(sec, GROUP) == 0, group < groups)
    is_last = lax.rem(sec, GROUP) == GROUP - 1
    far_next, far_prev = sec + GROUP < groups * GROUP, sec >= GROUP
    via_up = jnp.where(jnp.logical_and(is_last, far_next), group + 1, 0)
    via_dn = jnp.where(jnp.logical_and(is_first, far_prev), groups - group, 0)
    relay_up, relay_dn = jnp.logical_and(is_last, far_prev), jnp.logical_and(is_first, far_next)
    relays = jnp.where(relay_up, group, jnp.where(relay_dn, groups - 1 - group, 0))
    sections, _, rows, width = u_hbm.shape
    blocks, tiles = rows // BLOCK_ROWS, width // LANES
    lane = lax.broadcasted_iota(jnp.int32, (BLOCK_ROWS, LANES), 1)
    row = lax.broadcasted_iota(jnp.int32, (BLOCK_ROWS, LANES), 0)
    zero = jnp.float32(0.0)

    def rows_of(i):
        return pl.ds(BLOCK_ROWS * i, BLOCK_ROWS)

    def cols_of(j):
        return pl.ds(pl.multiple_of(j * LANES, LANES), LANES)

    def remote(src, dst, send, recv, device):
        return pltpu.make_async_remote_copy(
            src_ref=src, dst_ref=dst, send_sem=send, recv_sem=recv,
            device_id=device, device_id_type=pl.DeviceIdType.MESH,
        )

    barrier = pltpu.get_barrier_semaphore()
    phase = lax.rem(strip, 4)
    up_mutual, dn_mutual = jnp.logical_and(has_up, phase == 3), jnp.logical_and(has_dn, phase == 2)
    up_leads = jnp.logical_and(has_up, jnp.logical_or(phase == 1, phase == 2))
    dn_leads = jnp.logical_and(has_dn, phase == 3)
    up_follows = jnp.logical_and(has_up, phase == 0)
    dn_follows = jnp.logical_and(has_dn, phase < 2)

    def greet(exists, device):
        @pl.when(exists)
        def _():
            pl.semaphore_signal(
                barrier, inc=1, device_id=device, device_id_type=pl.DeviceIdType.MESH
            )

    def number(*conditions):
        return sum((x.astype(jnp.int32) for x in conditions), jnp.int32(0))

    greet(has_prev, prev_dev)
    greet(has_next, next_dev)
    far = [
        (jnp.logical_and(jnp.logical_or(is_first, is_last), far_next), {"sec": sec + GROUP}),
        (jnp.logical_and(jnp.logical_or(is_first, is_last), far_prev), {"sec": sec - GROUP}),
    ]
    if groups > 1:
        far.append((is_first, {"sec": sec + GROUP - 1}))
        far.append((is_last, {"sec": sec - GROUP + 1}))
    for exists, device in far:
        greet(exists, device)
    greet(up_mutual, up_dev)
    greet(dn_mutual, dn_dev)

    loads = [
        pltpu.make_async_copy(u_hbm, ub.at[0], local_sem.at[0]),
        pltpu.make_async_copy(c_hbm, cb, local_sem.at[1]),
        pltpu.make_async_copy(s_hbm, sho, local_sem.at[2]),
        pltpu.make_async_copy(w_hbm, wb, local_sem.at[3]),
    ]
    smalls = [
        pltpu.make_async_copy(class_hbm, class_k, local_sem.at[5]),
        pltpu.make_async_copy(cross_hbm, cross_k, local_sem.at[6]),
        pltpu.make_async_copy(fixed_hbm, fixed, local_sem.at[7]),
    ]
    for load in smalls + loads:
        load.start()

    def part(step, first, i):
        src = u_hbm if step == 0 else ub.at[1]
        return src.at[first:first + 2, :, rows_of(i), :]

    def to_prev(step, i):
        return remote(part(step, 0, i), nxt.at[step, :, :, rows_of(i), :],
                      dn_send.at[step, i], dn_recv.at[step, i], prev_dev)

    def to_next(step, i):
        return remote(part(step, 1, i), prv.at[step, :, :, rows_of(i), :],
                      up_send.at[step, i], up_recv.at[step, i], next_dev)

    def to_relay(step, i, up):
        return remote(part(step, 1 if up else 0, i), rel.at[step, i],
                      (up_send if up else dn_send).at[step, i], rel_recv.at[step, i],
                      {"sec": sec + GROUP if up else sec - GROUP})

    def from_relay(step, i, up):
        return remote(rel.at[step, i], (prv if up else nxt).at[step, :, :, rows_of(i), :],
                      rel_send.at[step, i], (up_recv if up else dn_recv).at[step, i],
                      {"sec": sec - GROUP + 1 if up else sec + GROUP - 1})

    def by_relay(step, i, count):
        return RELAYED[step].index(i) < count if i in RELAYED[step] else jnp.bool_(False)

    def send_chunk(step, i):
        @pl.when(jnp.logical_and(has_prev, jnp.logical_not(by_relay(step, i, via_dn))))
        def _():
            to_prev(step, i).start()

        @pl.when(jnp.logical_and(has_next, jnp.logical_not(by_relay(step, i, via_up))))
        def _():
            to_next(step, i).start()

    def send_by_relay(step, i):
        if i in RELAYED[step]:
            @pl.when(by_relay(step, i, via_dn))
            def _():
                to_relay(step, i, False).start()

            @pl.when(by_relay(step, i, via_up))
            def _():
                to_relay(step, i, True).start()

    def forward_first(n):
        for count in range(n + 1, len(RELAYED[0]) + 1):
            forward(0, RELAYED[0][count - 1 - n], relays == count)

    def forward(step, i, when=None):
        mine = by_relay(step, i, relays) if when is None else when

        @pl.when(mine)
        def _():
            to_relay(step, i, True).wait_recv()

        @pl.when(jnp.logical_and(mine, relay_up))
        def _():
            from_relay(step, i, True).start()

        @pl.when(jnp.logical_and(mine, relay_dn))
        def _():
            from_relay(step, i, False).start()

    def wait_chunk(step, i):
        @pl.when(has_next)
        def _():
            to_prev(step, i).wait_recv()

        @pl.when(has_prev)
        def _():
            to_next(step, i).wait_recv()

    def edge_to_dn(step):
        used = pl.ds(0, (3 if step == 0 else 2) * sections)
        return remote(edge_dn.at[step, used], edge_top.at[step, used],
                      edn_send.at[step], edn_recv.at[step], dn_dev)

    def edge_to_up(step):
        return remote(edge_up.at[step], edge_bot.at[step],
                      eup_send.at[step], eup_recv.at[step], up_dev)

    shifts_to_next = remote(s_hbm.at[1:3], shv, sh_send, sh_recv, next_dev)

    def stiffness(klass):
        table = [class_k[n] for n in range(CLASSES)]
        out = jnp.full(klass.shape, table[0], jnp.float32)
        for n in range(1, CLASSES):
            out = jnp.where(klass == n, table[n], out)
        return out

    def pack(step, last):
        dst, r = (edge_dn, rows - 1) if last else (edge_up, 0)
        for s in range(sections):
            for j in range(tiles):
                for c in range(2):
                    dst[step, 2 * s + c, pl.ds(j, 1), :] = ub[step, s, c, pl.ds(r, 1), pl.ds(j * LANES, LANES)]

    def send_edge(step, last, allowed):
        @pl.when(allowed)
        def _():
            (edge_to_dn if last else edge_to_up)(step).start()

    pl.semaphore_wait(
        barrier,
        number(has_prev, has_next, up_mutual, dn_mutual, up_leads, dn_leads, *(exists for exists, _ in far)),
    )
    for i in ORDER:
        send_by_relay(0, i)
    send_chunk(0, ORDER[0])
    for follows, leads, device in ((up_follows, up_leads, up_dev), (dn_follows, dn_leads, dn_dev)):
        greet(jnp.logical_or(follows, leads), device)

    @pl.when(has_next)
    def _():
        shifts_to_next.start()

    for load in smalls[:1] + loads[:2]:
        load.wait()
    pack(0, True)
    pack(0, False)
    for s in range(sections):
        for j in range(tiles):
            edge_class[s, pl.ds(j, 1), :] = cb[s, 1, pl.ds(rows - 1, 1), pl.ds(j * LANES, LANES)]
    for s in range(sections):
        edge_dn[0, 2 * sections + s] = stiffness(edge_class[s])

    send_edge(0, True, jnp.logical_or(dn_mutual, dn_leads))
    send_edge(0, False, jnp.logical_or(up_mutual, up_leads))
    for i in ORDER[1:3]:
        send_chunk(0, i)

    @pl.when(jnp.logical_not(has_prev))
    def _():
        prv[...] = jnp.zeros_like(prv)
        for a in range(2):
            for h in range(2):
                for i in range(blocks):
                    for j in range(tiles):
                        shp[a, h, i, j] = 0

    @pl.when(jnp.logical_not(has_next))
    def _():
        nxt[...] = jnp.zeros_like(nxt)

    @pl.when(jnp.logical_not(has_up))
    def _():
        edge_top[...] = jnp.zeros_like(edge_top)

    @pl.when(jnp.logical_not(has_dn))
    def _():
        edge_bot[...] = jnp.zeros_like(edge_bot)

    def vertical(step):
        @pl.loop(0, tiles)
        def _(j):
            cols = cols_of(j)
            inside = jnp.logical_or(lane < LANES - 1, j < tiles - 1)
            for s in range(sections):
                u = [[ub[step, s, c, rows_of(i), cols] for c in range(2)] for i in range(blocks)]
                turned = [[pltpu.roll(x, BLOCK_ROWS - 1, 0) for x in pair] for pair in u]
                from_above = None
                for i in range(blocks):
                    if step == 0:
                        kh[s, rows_of(i), cols] = jnp.where(inside, stiffness(cb[s, 0, rows_of(i), cols]), 0.0)
                        k = stiffness(cb[s, 1, rows_of(i), cols])
                        if i == blocks - 1:
                            k = jnp.where(row < BLOCK_ROWS - 1, k, 0.0)
                        kv[s, rows_of(i), cols] = k
                    else:
                        k = kv[s, rows_of(i), cols]
                    e = []
                    for c in range(2):
                        below = turned[i][c]
                        if i < blocks - 1:
                            below = jnp.where(row == BLOCK_ROWS - 1, turned[i + 1][c], below)
                        e.append(below - u[i][c])
                    f = pulled(e[0], e[1], k)
                    down = [pltpu.roll(x, 1, 0) for x in f]
                    for c in range(2):
                        before = 0.0 if from_above is None else from_above[c]
                        pf[s, c, rows_of(i), cols] = f[c] - jnp.where(row == 0, before, down[c])
                    from_above = down

    def ahead(pair, o):
        return [pltpu.roll(x, (-o) & (LANES - 1), 1) for x in pair]

    def behind(pair, o):
        return [pltpu.roll(x, o & (LANES - 1), 1) for x in pair]

    def inner(step, i):
        here = rows_of(i)

        def tile(j, carry):
            cols, right_cols = cols_of(j), cols_of(jnp.minimum(j + 1, tiles - 1))
            ahead_left, flow_left = carry
            u = [[ub[step, s, c, here, cols] for c in range(2)] for s in range(sections)]
            force = [[pf[s, c, here, cols] for c in range(2)] for s in range(sections)]
            new_ahead, new_flow = [], []
            for s in range(sections):
                e = []
                for c in range(2):
                    coming = pltpu.roll(ub[step, s, c, here, right_cols], LANES - 1, 1)
                    new_ahead.append(coming)
                    e.append(jnp.where(lane == LANES - 1, coming, ahead_left[2 * s + c]) - u[s][c])
                f = pulled(e[0], e[1], kh[s, here, cols])
                for c in range(2):
                    turned = pltpu.roll(f[c], 1, 1)
                    new_flow.append(turned)
                    force[s][c] += f[c] - jnp.where(lane == 0, flow_left[2 * s + c], turned)
            for s, h, k in ((0, 1, k1), (1, 1, k1), (0, 2, k2)):
                o = sho[s, h - 1, i, j]
                there = ahead(u[s + h], o)
                f = pulled(there[0] - u[s][0], there[1] - u[s][1], k)
                back = behind(f, o)
                for c in range(2):
                    force[s][c] += f[c]
                    force[s + h][c] -= back[c]
            for s in range(sections):
                for c in range(2):
                    pf[s, c, here, cols] = force[s][c]
            return tuple(new_ahead), tuple(new_flow)

        start = (
            tuple(
                pltpu.roll(ub[step, s, c, here, pl.ds(0, LANES)], LANES - 1, 1)
                for s in range(sections)
                for c in range(2)
            ),
            tuple(jnp.zeros((BLOCK_ROWS, LANES), jnp.float32) for _ in range(2 * sections)),
        )
        lax.fori_loop(0, tiles, tile, start, unroll=min(UNROLL, tiles))

    def edge(step, last):
        if last:
            @pl.when(has_dn)
            def _():
                edge_to_up(step).wait_recv()
        else:
            @pl.when(has_up)
            def _():
                edge_to_dn(step).wait_recv()
        mine, theirs = (edge_dn, edge_bot) if last else (edge_up, edge_top)
        for s in range(sections):
            k = jnp.where(has_dn, edge_dn[0, 2 * sections + s], zero) if last else edge_top[0, 2 * sections + s]
            e = [theirs[step, 2 * s + c] - mine[step, 2 * s + c] for c in range(2)]
            f = pulled(e[0], e[1], k)
            for c in range(2):
                edge_flow[2 * s + c] = f[c]

    def outer(step, i):
        here = rows_of(i)
        edge_row = {0: 0, blocks - 1: BLOCK_ROWS - 1}.get(i)

        def tile(j, carry):
            cols = cols_of(j)
            u = [[ub[step, s, c, here, cols] for c in range(2)] for s in range(sections)]
            force = [[pf[s, c, here, cols] for c in range(2)] for s in range(sections)]
            if edge_row is not None:
                for s in range(sections):
                    for c in range(2):
                        f = jnp.broadcast_to(edge_flow[2 * s + c, pl.ds(j, 1), :], (BLOCK_ROWS, LANES))
                        force[s][c] += jnp.where(row == edge_row, f, 0.0)
            after = [[nxt[step, s, c, here, cols] for c in range(2)] for s in range(2)]
            for s, h, t, k in ((2, 1, 0, k1n), (1, 2, 0, k2n), (2, 2, 1, k2n)):
                there = ahead(after[t], sho[s, h - 1, i, j])
                f = pulled(there[0] - u[s][0], there[1] - u[s][1], k)
                for c in range(2):
                    force[s][c] += f[c]
            before = [[prv[step, s, c, here, cols] for c in range(2)] for s in range(2)]
            for t, h, s, k in ((1, 1, 0, k1p), (0, 2, 0, k2p), (1, 2, 1, k2p)):
                there = behind(before[t], shp[t, h - 1, i, j])
                f = pulled(there[0] - u[s][0], there[1] - u[s][1], k)
                for c in range(2):
                    force[s][c] += f[c]
            for s in range(sections):
                for c in range(2):
                    speed = (DAMPING * wb[s, c, here, cols] + TIME_STEP * force[s][c]) * moving[s]
                    moved = u[s][c] + TIME_STEP * speed
                    if step == 0:
                        wb[s, c, here, cols] = speed
                        ub[1, s, c, here, cols] = moved
                    else:
                        ow[s, c, here, cols] = speed
                        ou[s, c, here, cols] = moved
            return carry

        lax.fori_loop(0, tiles, tile, 0, unroll=min(UNROLL, tiles))

    for load in smalls[1:]:
        load.wait()
    k1, k2 = cross_k[0], cross_k[1]
    k1n, k2n = jnp.where(has_next, k1, zero), jnp.where(has_next, k2, zero)
    k1p, k2p = jnp.where(has_prev, k1, zero), jnp.where(has_prev, k2, zero)
    moving = [jnp.where(fixed[s] == 0, jnp.float32(1.0), zero) for s in range(sections)]

    for step in range(2):
        vertical(step)
        if step == 0:
            loads[2].wait()
        for n, i in enumerate(ORDER):
            inner(step, i)
            if step == 0 and n == 0:
                loads[3].wait()

                @pl.when(has_prev)
                def _():
                    shifts_to_next.wait_recv()
                    fetch = pltpu.make_async_copy(shv, shp, local_sem.at[4])
                    fetch.start()
                    fetch.wait()

                forward_first(0)
            elif step == 0 and n == 1:
                forward_first(2)
            elif step == 0 and n == 3:
                forward(1, RELAYED[1][0])
            elif step == 1 and n == 0:
                forward(1, RELAYED[1][2])

            if i in (0, blocks - 1):
                edge(step, i != 0)
            wait_chunk(step, i)
            outer(step, i)
            if step == 0:
                send_by_relay(1, i)
                if n == 0:
                    forward_first(1)

                    @pl.when(jnp.logical_or(up_follows, dn_follows))
                    def _():
                        pl.semaphore_wait(barrier, number(up_follows, dn_follows))

                    send_edge(0, True, dn_follows)
                    send_edge(0, False, up_follows)
                if i in (0, blocks - 1):
                    pack(1, i != 0)
                    send_edge(1, i != 0, has_dn if i else has_up)
                if n == 1:
                    send_chunk(0, ORDER[3])
                    send_chunk(1, ORDER[0])
                elif n == 2:
                    send_chunk(1, ORDER[1])
                    send_chunk(1, ORDER[2])
                    forward(1, RELAYED[1][1])
                elif n == 3:
                    send_chunk(1, ORDER[3])

    for step in range(2):
        for i in RELAYED[step]:
            @pl.when(by_relay(step, i, relays))
            def _():
                from_relay(step, i, True).wait_send()

        for i in range(blocks):
            @pl.when(has_prev)
            def _():
                to_prev(step, i).wait_send()

            @pl.when(has_next)
            def _():
                to_next(step, i).wait_send()

        @pl.when(has_dn)
        def _():
            edge_to_dn(step).wait_send()

        @pl.when(has_up)
        def _():
            edge_to_up(step).wait_send()

    @pl.when(has_next)
    def _():
        shifts_to_next.wait_send()


def store(ou, ow, pos, vel, sem):
    copies = []
    for k, (src, dst) in enumerate(((ou, pos), (ow, vel))):
        for s in range(src.shape[0]):
            copies.append(pltpu.make_async_copy(src.at[s], dst.at[s], sem.at[k, s]))
    for copy in copies:
        copy.start()
    for copy in copies:
        copy.wait()


def per_device(positions, velocity, spring_class, match_shift, fixed, class_stiffness, cross_stiffness):
    sections, comps, rows, width = positions.shape
    blocks, tiles = rows // BLOCK_ROWS, width // LANES
    full = (sections, comps, rows, width)
    f32, i32 = jnp.float32, jnp.int32
    any_spec = pl.BlockSpec(memory_space=pl.ANY)
    smem_spec = pl.BlockSpec(memory_space=pltpu.SMEM)
    vmem_spec = pl.BlockSpec(memory_space=pltpu.VMEM)
    dma = pltpu.SemaphoreType.DMA
    moved, speed = pl.pallas_call(
        kernel,
        out_shape=(pltpu.VMEM(full, f32), pltpu.VMEM(full, f32)),
        in_specs=[any_spec] * 7,
        out_specs=(vmem_spec, vmem_spec),
        scratch_shapes=[
            pltpu.SMEM((sections,), i32), pltpu.SMEM((CLASSES,), f32), pltpu.SMEM((2,), f32),
            pltpu.VMEM((2,) + full, f32),
            pltpu.VMEM(full, f32),
            pltpu.VMEM(full, i32),
            pltpu.VMEM((sections, rows, width), f32),
            pltpu.VMEM((sections, rows, width), f32),
            pltpu.VMEM(full, f32),
            pltpu.VMEM((2, 2, comps, rows, width), f32),
            pltpu.VMEM((2, 2, comps, rows, width), f32),
            pltpu.VMEM((2, blocks, 2, comps, BLOCK_ROWS, width), f32),
            pltpu.VMEM((2, 3 * sections, tiles, LANES), f32),
            pltpu.VMEM((2, 2 * sections, tiles, LANES), f32),
            pltpu.VMEM((2, 3 * sections, tiles, LANES), f32),
            pltpu.VMEM((2, 2 * sections, tiles, LANES), f32),
            pltpu.VMEM((sections, tiles, LANES), i32),
            pltpu.VMEM((2 * sections, tiles, LANES), f32),
            pltpu.VMEM((2, 2, blocks, tiles), i32),
            pltpu.SMEM((2, 2, blocks, tiles), i32),
            pltpu.SMEM((sections, 2, blocks, tiles), i32),
            dma((8,)),
            dma((2, blocks)), dma((2, blocks)), dma((2, blocks)), dma((2, blocks)),
            dma((2, blocks)), dma((2, blocks)),
            dma((2,)), dma((2,)), dma((2,)), dma((2,)), dma(()), dma(()),
        ],
        compiler_params=pltpu.CompilerParams(collective_id=0, has_side_effects=True),
        name="relax",
    )(positions, velocity, spring_class, match_shift, fixed, class_stiffness, cross_stiffness)
    moved = pltpu.with_memory_space_constraint(moved, pltpu.VMEM)
    speed = pltpu.with_memory_space_constraint(speed, pltpu.VMEM)
    return pl.pallas_call(
        store,
        out_shape=(jax.ShapeDtypeStruct(full, f32), jax.ShapeDtypeStruct(full, f32)),
        in_specs=[vmem_spec] * 2,
        out_specs=(any_spec, any_spec),
        scratch_shapes=[dma((2, sections))],
        name="store",
    )(moved, speed)


def solution(mesh):
    grid = P("sec", None, "strip", None)
    return jax.shard_map(
        per_device,
        mesh=mesh,
        in_specs=(grid, grid, grid, grid, P("sec"), P(), P()),
        out_specs=(grid, grid),
        check_vma=False,
    )
```

```python
import jax
import jax.numpy as jnp
from jax import lax
from jax.experimental import pallas as pl
from jax.experimental.pallas import tpu as pltpu
from jax.sharding import PartitionSpec as P

BLOCK_ROWS = 8
LANES = 128
CLASSES = 8
DAMPING = 0.9
TIME_STEP = 0.35
ORDER = (1, 3, 0, 2)
RELAYED = ((2, 0, 3), (3, 1, 0))
PARTS = 2
GROUP = 4
UNROLL = 4


def pulled(ex, ey, k):
    r = 1.0 / (1.0 + (ex * ex + ey * ey))
    g = k * (1.5 - 0.5 * r)
    return ex * g, ey * g


def kernel(
    u_hbm, w_hbm, c_hbm, s_hbm, fixed_hbm, class_hbm, cross_hbm, ou, ow, fixed, class_k, cross_k,
    ub, wb, cb, kh, kv, pf, nxt, prv, rel,
    edge_dn, edge_up, edge_top, edge_bot, edge_class, edge_flow, shv, shp, sho,
    local_sem, dn_send, dn_recv, up_send, up_recv,
    rel_send, rel_recv, edn_send, edn_recv, eup_send, eup_recv, sh_send, sh_recv,
):
    n_sec, n_strip = lax.axis_size("sec"), lax.axis_size("strip")
    sec, strip = lax.axis_index("sec"), lax.axis_index("strip")
    has_prev, has_next = sec > 0, sec < n_sec - 1
    has_up, has_dn = strip > 0, strip < n_strip - 1
    prev_dev, next_dev = {"sec": sec - 1}, {"sec": sec + 1}
    up_dev, dn_dev = {"strip": strip - 1}, {"strip": strip + 1}
    groups, group = n_sec // GROUP, sec // GROUP
    is_first = jnp.logical_and(lax.rem(sec, GROUP) == 0, group < groups)
    is_last = lax.rem(sec, GROUP) == GROUP - 1
    far_next, far_prev = sec + GROUP < groups * GROUP, sec >= GROUP
    via_up = jnp.where(jnp.logical_and(is_last, far_next), group + 1, 0)
    via_dn = jnp.where(jnp.logical_and(is_first, far_prev), groups - group, 0)
    relay_up, relay_dn = jnp.logical_and(is_last, far_prev), jnp.logical_and(is_first, far_next)
    relays = jnp.where(relay_up, group, jnp.where(relay_dn, groups - 1 - group, 0))
    sections, _, rows, width = u_hbm.shape
    blocks, tiles = rows // BLOCK_ROWS, width // LANES
    lane = lax.broadcasted_iota(jnp.int32, (BLOCK_ROWS, LANES), 1)
    row = lax.broadcasted_iota(jnp.int32, (BLOCK_ROWS, LANES), 0)
    zero = jnp.float32(0.0)

    def rows_of(i):
        return pl.ds(BLOCK_ROWS * i, BLOCK_ROWS)

    def span_of(p):
        return pl.ds(p * (width // PARTS), width // PARTS)

    def cols_of(j):
        return pl.ds(pl.multiple_of(j * LANES, LANES), LANES)

    def remote(src, dst, send, recv, device):
        return pltpu.make_async_remote_copy(
            src_ref=src, dst_ref=dst, send_sem=send, recv_sem=recv,
            device_id=device, device_id_type=pl.DeviceIdType.MESH,
        )

    barrier = pltpu.get_barrier_semaphore()
    phase = lax.rem(strip, 4)
    up_mutual, dn_mutual = jnp.logical_and(has_up, phase == 3), jnp.logical_and(has_dn, phase == 2)
    up_leads = jnp.logical_and(has_up, jnp.logical_or(phase == 1, phase == 2))
    dn_leads = jnp.logical_and(has_dn, phase == 3)
    up_follows = jnp.logical_and(has_up, phase == 0)
    dn_follows = jnp.logical_and(has_dn, phase < 2)

    def greet(exists, device):
        @pl.when(exists)
        def _():
            pl.semaphore_signal(
                barrier, inc=1, device_id=device, device_id_type=pl.DeviceIdType.MESH
            )

    def number(*conditions):
        return sum((x.astype(jnp.int32) for x in conditions), jnp.int32(0))

    greet(has_prev, prev_dev)
    greet(has_next, next_dev)
    far = [
        (jnp.logical_and(jnp.logical_or(is_first, is_last), far_next), {"sec": sec + GROUP}),
        (jnp.logical_and(jnp.logical_or(is_first, is_last), far_prev), {"sec": sec - GROUP}),
    ]
    if groups > 1:
        far.append((is_first, {"sec": sec + GROUP - 1}))
        far.append((is_last, {"sec": sec - GROUP + 1}))
    for exists, device in far:
        greet(exists, device)
    greet(up_mutual, up_dev)
    greet(dn_mutual, dn_dev)

    loads = [
        pltpu.make_async_copy(u_hbm, ub.at[0], local_sem.at[0]),
        pltpu.make_async_copy(c_hbm, cb, local_sem.at[1]),
        pltpu.make_async_copy(s_hbm, sho, local_sem.at[2]),
        pltpu.make_async_copy(w_hbm, wb, local_sem.at[3]),
    ]
    smalls = [
        pltpu.make_async_copy(class_hbm, class_k, local_sem.at[5]),
        pltpu.make_async_copy(cross_hbm, cross_k, local_sem.at[6]),
        pltpu.make_async_copy(fixed_hbm, fixed, local_sem.at[7]),
    ]
    for load in smalls + loads:
        load.start()

    chunks = [(i, p) for i in ORDER for p in range(PARTS)]
    relayed = [[(i, p) for i in RELAYED[step] for p in reversed(range(PARTS))] for step in range(2)]

    def source(step, first, i, p):
        src = u_hbm if step == 0 else ub.at[1]
        return src.at[first:first + 2, :, rows_of(i), span_of(p)]

    def to_prev(step, i, p):
        return remote(source(step, 0, i, p), nxt.at[step, :, :, rows_of(i), span_of(p)],
                      dn_send.at[step, i, p], dn_recv.at[step, i, p], prev_dev)

    def to_next(step, i, p):
        return remote(source(step, 1, i, p), prv.at[step, :, :, rows_of(i), span_of(p)],
                      up_send.at[step, i, p], up_recv.at[step, i, p], next_dev)

    def to_relay(step, i, p, up):
        return remote(source(step, 1 if up else 0, i, p), rel.at[step, i, p],
                      (up_send if up else dn_send).at[step, i, p], rel_recv.at[step, i, p],
                      {"sec": sec + GROUP if up else sec - GROUP})

    def from_relay(step, i, p, up):
        return remote(rel.at[step, i, p], (prv if up else nxt).at[step, :, :, rows_of(i), span_of(p)],
                      rel_send.at[step, i, p], (up_recv if up else dn_recv).at[step, i, p],
                      {"sec": sec - GROUP + 1 if up else sec + GROUP - 1})

    def by_relay(step, i, p, count):
        if (i, p) not in relayed[step]:
            return jnp.bool_(False)
        return relayed[step].index((i, p)) < PARTS * count

    def send_chunk(step, i, p):
        @pl.when(jnp.logical_and(has_prev, jnp.logical_not(by_relay(step, i, p, via_dn))))
        def _():
            to_prev(step, i, p).start()

        @pl.when(jnp.logical_and(has_next, jnp.logical_not(by_relay(step, i, p, via_up))))
        def _():
            to_next(step, i, p).start()

    def send_by_relay(step, i, p):
        if (i, p) in relayed[step]:
            @pl.when(by_relay(step, i, p, via_dn))
            def _():
                to_relay(step, i, p, False).start()

            @pl.when(by_relay(step, i, p, via_up))
            def _():
                to_relay(step, i, p, True).start()

    def forward_first(n):
        for count in range(n // PARTS + 1, len(RELAYED[0]) + 1):
            forward(0, *relayed[0][PARTS * count - 1 - n], relays == count)

    def forward(step, i, p, when=None):
        mine = by_relay(step, i, p, relays) if when is None else when

        @pl.when(mine)
        def _():
            to_relay(step, i, p, True).wait_recv()

        @pl.when(jnp.logical_and(mine, relay_up))
        def _():
            from_relay(step, i, p, True).start()

        @pl.when(jnp.logical_and(mine, relay_dn))
        def _():
            from_relay(step, i, p, False).start()

    def wait_chunk(step, i, p):
        @pl.when(has_next)
        def _():
            to_prev(step, i, p).wait_recv()

        @pl.when(has_prev)
        def _():
            to_next(step, i, p).wait_recv()

    def edge_to_dn(step):
        used = pl.ds(0, (3 if step == 0 else 2) * sections)
        return remote(edge_dn.at[step, used], edge_top.at[step, used],
                      edn_send.at[step], edn_recv.at[step], dn_dev)

    def edge_to_up(step):
        return remote(edge_up.at[step], edge_bot.at[step],
                      eup_send.at[step], eup_recv.at[step], up_dev)

    shifts_to_next = remote(s_hbm.at[1:3], shv, sh_send, sh_recv, next_dev)

    def stiffness(klass):
        table = [class_k[n] for n in range(CLASSES)]
        out = jnp.full(klass.shape, table[0], jnp.float32)
        for n in range(1, CLASSES):
            out = jnp.where(klass == n, table[n], out)
        return out

    def pack(step, last):
        dst, r = (edge_dn, rows - 1) if last else (edge_up, 0)
        for s in range(sections):
            for j in range(tiles):
                for c in range(2):
                    dst[step, 2 * s + c, pl.ds(j, 1), :] = ub[step, s, c, pl.ds(r, 1), pl.ds(j * LANES, LANES)]

    def send_edge(step, last, allowed):
        @pl.when(allowed)
        def _():
            (edge_to_dn if last else edge_to_up)(step).start()

    pl.semaphore_wait(
        barrier,
        number(has_prev, has_next, up_mutual, dn_mutual, up_leads, dn_leads, *(exists for exists, _ in far)),
    )
    for chunk in chunks:
        send_by_relay(0, *chunk)
    send_chunk(0, *chunks[0])
    for follows, leads, device in ((up_follows, up_leads, up_dev), (dn_follows, dn_leads, dn_dev)):
        greet(jnp.logical_or(follows, leads), device)

    @pl.when(has_next)
    def _():
        shifts_to_next.start()

    for load in smalls[:1] + loads[:2]:
        load.wait()
    pack(0, True)
    pack(0, False)
    for s in range(sections):
        for j in range(tiles):
            edge_class[s, pl.ds(j, 1), :] = cb[s, 1, pl.ds(rows - 1, 1), pl.ds(j * LANES, LANES)]
    for s in range(sections):
        edge_dn[0, 2 * sections + s] = stiffness(edge_class[s])

    send_edge(0, True, jnp.logical_or(dn_mutual, dn_leads))
    send_edge(0, False, jnp.logical_or(up_mutual, up_leads))
    for chunk in chunks[1:]:
        send_chunk(0, *chunk)

    @pl.when(jnp.logical_not(has_prev))
    def _():
        prv[...] = jnp.zeros_like(prv)
        for a in range(2):
            for h in range(2):
                for i in range(blocks):
                    for j in range(tiles):
                        shp[a, h, i, j] = 0

    @pl.when(jnp.logical_not(has_next))
    def _():
        nxt[...] = jnp.zeros_like(nxt)

    @pl.when(jnp.logical_not(has_up))
    def _():
        edge_top[...] = jnp.zeros_like(edge_top)

    @pl.when(jnp.logical_not(has_dn))
    def _():
        edge_bot[...] = jnp.zeros_like(edge_bot)

    def vertical(step):
        @pl.loop(0, tiles)
        def _(j):
            cols = cols_of(j)
            inside = jnp.logical_or(lane < LANES - 1, j < tiles - 1)
            for s in range(sections):
                u = [[ub[step, s, c, rows_of(i), cols] for c in range(2)] for i in range(blocks)]
                turned = [[pltpu.roll(x, BLOCK_ROWS - 1, 0) for x in pair] for pair in u]
                from_above = None
                for i in range(blocks):
                    if step == 0:
                        kh[s, rows_of(i), cols] = jnp.where(inside, stiffness(cb[s, 0, rows_of(i), cols]), 0.0)
                        k = stiffness(cb[s, 1, rows_of(i), cols])
                        if i == blocks - 1:
                            k = jnp.where(row < BLOCK_ROWS - 1, k, 0.0)
                        kv[s, rows_of(i), cols] = k
                    else:
                        k = kv[s, rows_of(i), cols]
                    e = []
                    for c in range(2):
                        below = turned[i][c]
                        if i < blocks - 1:
                            below = jnp.where(row == BLOCK_ROWS - 1, turned[i + 1][c], below)
                        e.append(below - u[i][c])
                    f = pulled(e[0], e[1], k)
                    down = [pltpu.roll(x, 1, 0) for x in f]
                    for c in range(2):
                        before = 0.0 if from_above is None else from_above[c]
                        pf[s, c, rows_of(i), cols] = f[c] - jnp.where(row == 0, before, down[c])
                    from_above = down

    def ahead(pair, o):
        return [pltpu.roll(x, (-o) & (LANES - 1), 1) for x in pair]

    def behind(pair, o):
        return [pltpu.roll(x, o & (LANES - 1), 1) for x in pair]

    def inner(step, i):
        here = rows_of(i)

        def tile(j, carry):
            cols, right_cols = cols_of(j), cols_of(jnp.minimum(j + 1, tiles - 1))
            ahead_left, flow_left = carry
            u = [[ub[step, s, c, here, cols] for c in range(2)] for s in range(sections)]
            force = [[pf[s, c, here, cols] for c in range(2)] for s in range(sections)]
            new_ahead, new_flow = [], []
            for s in range(sections):
                e = []
                for c in range(2):
                    coming = pltpu.roll(ub[step, s, c, here, right_cols], LANES - 1, 1)
                    new_ahead.append(coming)
                    e.append(jnp.where(lane == LANES - 1, coming, ahead_left[2 * s + c]) - u[s][c])
                f = pulled(e[0], e[1], kh[s, here, cols])
                for c in range(2):
                    turned = pltpu.roll(f[c], 1, 1)
                    new_flow.append(turned)
                    force[s][c] += f[c] - jnp.where(lane == 0, flow_left[2 * s + c], turned)
            for s, h, k in ((0, 1, k1), (1, 1, k1), (0, 2, k2)):
                o = sho[s, h - 1, i, j]
                there = ahead(u[s + h], o)
                f = pulled(there[0] - u[s][0], there[1] - u[s][1], k)
                back = behind(f, o)
                for c in range(2):
                    force[s][c] += f[c]
                    force[s + h][c] -= back[c]
            for s in range(sections):
                for c in range(2):
                    pf[s, c, here, cols] = force[s][c]
            return tuple(new_ahead), tuple(new_flow)

        start = (
            tuple(
                pltpu.roll(ub[step, s, c, here, pl.ds(0, LANES)], LANES - 1, 1)
                for s in range(sections)
                for c in range(2)
            ),
            tuple(jnp.zeros((BLOCK_ROWS, LANES), jnp.float32) for _ in range(2 * sections)),
        )
        lax.fori_loop(0, tiles, tile, start, unroll=min(UNROLL, tiles))

    def edge(step, last):
        if last:
            @pl.when(has_dn)
            def _():
                edge_to_up(step).wait_recv()
        else:
            @pl.when(has_up)
            def _():
                edge_to_dn(step).wait_recv()
        mine, theirs = (edge_dn, edge_bot) if last else (edge_up, edge_top)
        for s in range(sections):
            k = jnp.where(has_dn, edge_dn[0, 2 * sections + s], zero) if last else edge_top[0, 2 * sections + s]
            e = [theirs[step, 2 * s + c] - mine[step, 2 * s + c] for c in range(2)]
            f = pulled(e[0], e[1], k)
            for c in range(2):
                edge_flow[2 * s + c] = f[c]

    def outer(step, i, p):
        here = rows_of(i)
        edge_row = {0: 0, blocks - 1: BLOCK_ROWS - 1}.get(i)

        def tile(j, carry):
            cols = cols_of(j)
            u = [[ub[step, s, c, here, cols] for c in range(2)] for s in range(sections)]
            force = [[pf[s, c, here, cols] for c in range(2)] for s in range(sections)]
            if edge_row is not None:
                for s in range(sections):
                    for c in range(2):
                        f = jnp.broadcast_to(edge_flow[2 * s + c, pl.ds(j, 1), :], (BLOCK_ROWS, LANES))
                        force[s][c] += jnp.where(row == edge_row, f, 0.0)
            after = [[nxt[step, s, c, here, cols] for c in range(2)] for s in range(2)]
            for s, h, t, k in ((2, 1, 0, k1n), (1, 2, 0, k2n), (2, 2, 1, k2n)):
                there = ahead(after[t], sho[s, h - 1, i, j])
                f = pulled(there[0] - u[s][0], there[1] - u[s][1], k)
                for c in range(2):
                    force[s][c] += f[c]
            before = [[prv[step, s, c, here, cols] for c in range(2)] for s in range(2)]
            for t, h, s, k in ((1, 1, 0, k1p), (0, 2, 0, k2p), (1, 2, 1, k2p)):
                there = behind(before[t], shp[t, h - 1, i, j])
                f = pulled(there[0] - u[s][0], there[1] - u[s][1], k)
                for c in range(2):
                    force[s][c] += f[c]
            for s in range(sections):
                for c in range(2):
                    speed = (DAMPING * wb[s, c, here, cols] + TIME_STEP * force[s][c]) * moving[s]
                    moved = u[s][c] + TIME_STEP * speed
                    if step == 0:
                        wb[s, c, here, cols] = speed
                        ub[1, s, c, here, cols] = moved
                    else:
                        ow[s, c, here, cols] = speed
                        ou[s, c, here, cols] = moved
            return carry

        lax.fori_loop(p * tiles // PARTS, (p + 1) * tiles // PARTS, tile, 0, unroll=min(UNROLL, tiles // PARTS))

    for load in smalls[1:]:
        load.wait()
    k1, k2 = cross_k[0], cross_k[1]
    k1n, k2n = jnp.where(has_next, k1, zero), jnp.where(has_next, k2, zero)
    k1p, k2p = jnp.where(has_prev, k1, zero), jnp.where(has_prev, k2, zero)
    moving = [jnp.where(fixed[s] == 0, jnp.float32(1.0), zero) for s in range(sections)]

    for step in range(2):
        vertical(step)
        if step == 0:
            loads[2].wait()
        for n, i in enumerate(ORDER):
            inner(step, i)
            if step == 0 and n == 0:
                loads[3].wait()

                @pl.when(has_prev)
                def _():
                    shifts_to_next.wait_recv()
                    fetch = pltpu.make_async_copy(shv, shp, local_sem.at[4])
                    fetch.start()
                    fetch.wait()

            if i in (0, blocks - 1):
                edge(step, i != 0)
            for p in range(PARTS):
                if step == 0 and n < 3:
                    m = n * PARTS + p
                    for k in (0, 1) if m == 0 else (m + 1,):
                        if k < PARTS * len(RELAYED[0]):
                            forward_first(k)
                elif step == 0 and n == 3:
                    forward(1, RELAYED[1][0], p)
                elif step == 1 and n == 0:
                    forward(1, RELAYED[1][2], p)
                wait_chunk(step, i, p)
                outer(step, i, p)
                if step == 0:
                    send_by_relay(1, i, p)
                    if n == 3:
                        send_chunk(1, i, p)
            if step == 0:
                if n == 0:
                    @pl.when(jnp.logical_or(up_follows, dn_follows))
                    def _():
                        pl.semaphore_wait(barrier, number(up_follows, dn_follows))

                    send_edge(0, True, dn_follows)
                    send_edge(0, False, up_follows)
                if i in (0, blocks - 1):
                    pack(1, i != 0)
                    send_edge(1, i != 0, has_dn if i else has_up)
                if n == 1:
                    for chunk in chunks[:PARTS]:
                        send_chunk(1, *chunk)
                elif n == 2:
                    for chunk in chunks[PARTS:3 * PARTS]:
                        send_chunk(1, *chunk)
                    for p in range(PARTS):
                        forward(1, RELAYED[1][1], p)

    for step in range(2):
        for chunk in relayed[step]:
            @pl.when(by_relay(step, *chunk, relays))
            def _():
                from_relay(step, *chunk, True).wait_send()

        for chunk in chunks:
            @pl.when(has_prev)
            def _():
                to_prev(step, *chunk).wait_send()

            @pl.when(has_next)
            def _():
                to_next(step, *chunk).wait_send()

        @pl.when(has_dn)
        def _():
            edge_to_dn(step).wait_send()

        @pl.when(has_up)
        def _():
            edge_to_up(step).wait_send()

    @pl.when(has_next)
    def _():
        shifts_to_next.wait_send()


def store(ou, ow, pos, vel, sem):
    copies = []
    for k, (src, dst) in enumerate(((ou, pos), (ow, vel))):
        for s in range(src.shape[0]):
            copies.append(pltpu.make_async_copy(src.at[s], dst.at[s], sem.at[k, s]))
    for copy in copies:
        copy.start()
    for copy in copies:
        copy.wait()


def per_device(positions, velocity, spring_class, match_shift, fixed, class_stiffness, cross_stiffness):
    sections, comps, rows, width = positions.shape
    blocks, tiles = rows // BLOCK_ROWS, width // LANES
    full = (sections, comps, rows, width)
    f32, i32 = jnp.float32, jnp.int32
    any_spec = pl.BlockSpec(memory_space=pl.ANY)
    smem_spec = pl.BlockSpec(memory_space=pltpu.SMEM)
    vmem_spec = pl.BlockSpec(memory_space=pltpu.VMEM)
    dma = pltpu.SemaphoreType.DMA
    moved, speed = pl.pallas_call(
        kernel,
        out_shape=(pltpu.VMEM(full, f32), pltpu.VMEM(full, f32)),
        in_specs=[any_spec] * 7,
        out_specs=(vmem_spec, vmem_spec),
        scratch_shapes=[
            pltpu.SMEM((sections,), i32), pltpu.SMEM((CLASSES,), f32), pltpu.SMEM((2,), f32),
            pltpu.VMEM((2,) + full, f32),
            pltpu.VMEM(full, f32),
            pltpu.VMEM(full, i32),
            pltpu.VMEM((sections, rows, width), f32),
            pltpu.VMEM((sections, rows, width), f32),
            pltpu.VMEM(full, f32),
            pltpu.VMEM((2, 2, comps, rows, width), f32),
            pltpu.VMEM((2, 2, comps, rows, width), f32),
            pltpu.VMEM((2, blocks, PARTS, 2, comps, BLOCK_ROWS, width // PARTS), f32),
            pltpu.VMEM((2, 3 * sections, tiles, LANES), f32),
            pltpu.VMEM((2, 2 * sections, tiles, LANES), f32),
            pltpu.VMEM((2, 3 * sections, tiles, LANES), f32),
            pltpu.VMEM((2, 2 * sections, tiles, LANES), f32),
            pltpu.VMEM((sections, tiles, LANES), i32),
            pltpu.VMEM((2 * sections, tiles, LANES), f32),
            pltpu.VMEM((2, 2, blocks, tiles), i32),
            pltpu.SMEM((2, 2, blocks, tiles), i32),
            pltpu.SMEM((sections, 2, blocks, tiles), i32),
            dma((8,)),
            *[dma((2, blocks, PARTS)) for _ in range(6)],
            dma((2,)), dma((2,)), dma((2,)), dma((2,)), dma(()), dma(()),
        ],
        compiler_params=pltpu.CompilerParams(collective_id=0, has_side_effects=True),
        name="relax",
    )(positions, velocity, spring_class, match_shift, fixed, class_stiffness, cross_stiffness)
    moved = pltpu.with_memory_space_constraint(moved, pltpu.VMEM)
    speed = pltpu.with_memory_space_constraint(speed, pltpu.VMEM)
    return pl.pallas_call(
        store,
        out_shape=(jax.ShapeDtypeStruct(full, f32), jax.ShapeDtypeStruct(full, f32)),
        in_specs=[vmem_spec] * 2,
        out_specs=(any_spec, any_spec),
        scratch_shapes=[dma((2, sections))],
        name="store",
    )(moved, speed)


def solution(mesh):
    grid = P("sec", None, "strip", None)
    return jax.shard_map(
        per_device,
        mesh=mesh,
        in_specs=(grid, grid, grid, grid, P("sec"), P(), P()),
        out_specs=(grid, grid),
        check_vma=False,
    )
```

```python
import jax
import jax.numpy as jnp
from jax import lax
from jax.experimental import pallas as pl
from jax.experimental.pallas import tpu as pltpu
from jax.sharding import PartitionSpec as P

BLOCK_ROWS = 8
LANES = 128
CLASSES = 8
DAMPING = 0.9
TIME_STEP = 0.35
ORDER = (1, 3, 0, 2)
RELAYED = ((2, 0, 3), (3, 1, 0))
PARTS = 2
GROUP = 4
UNROLL = 4


def pulled(ex, ey, k):
    r = 1.0 / (1.0 + (ex * ex + ey * ey))
    g = k * (1.5 - 0.5 * r)
    return ex * g, ey * g


def kernel(
    u_hbm, w_hbm, c_hbm, s_hbm, fixed_hbm, class_hbm, cross_hbm, ou, ow, fixed, class_k, cross_k,
    ub, wb, cb, kh, kv, pf, nxt, prv, rel,
    edge_dn, edge_up, edge_top, edge_bot, edge_class, edge_flow, shv, shp, sho,
    local_sem, dn_send, dn_recv, up_send, up_recv,
    rel_send, rel_recv, edn_send, edn_recv, eup_send, eup_recv, sh_send, sh_recv,
):
    n_sec, n_strip = lax.axis_size("sec"), lax.axis_size("strip")
    sec, strip = lax.axis_index("sec"), lax.axis_index("strip")
    has_prev, has_next = sec > 0, sec < n_sec - 1
    has_up, has_dn = strip > 0, strip < n_strip - 1
    prev_dev, next_dev = {"sec": sec - 1}, {"sec": sec + 1}
    up_dev, dn_dev = {"strip": strip - 1}, {"strip": strip + 1}
    groups, group = n_sec // GROUP, sec // GROUP
    is_first = jnp.logical_and(lax.rem(sec, GROUP) == 0, group < groups)
    is_last = lax.rem(sec, GROUP) == GROUP - 1
    far_next, far_prev = sec + GROUP < groups * GROUP, sec >= GROUP
    via_up = jnp.where(jnp.logical_and(is_last, far_next), group + 1, 0)
    via_dn = jnp.where(jnp.logical_and(is_first, far_prev), groups - group, 0)
    relay_up, relay_dn = jnp.logical_and(is_last, far_prev), jnp.logical_and(is_first, far_next)
    relays = jnp.where(relay_up, group, jnp.where(relay_dn, groups - 1 - group, 0))
    sections, _, rows, width = u_hbm.shape
    blocks, tiles = rows // BLOCK_ROWS, width // LANES
    lane = lax.broadcasted_iota(jnp.int32, (BLOCK_ROWS, LANES), 1)
    row = lax.broadcasted_iota(jnp.int32, (BLOCK_ROWS, LANES), 0)
    zero = jnp.float32(0.0)

    def rows_of(i):
        return pl.ds(BLOCK_ROWS * i, BLOCK_ROWS)

    def span_of(p):
        return pl.ds(p * (width // PARTS), width // PARTS)

    def cols_of(j):
        return pl.ds(pl.multiple_of(j * LANES, LANES), LANES)

    def remote(src, dst, send, recv, device):
        return pltpu.make_async_remote_copy(
            src_ref=src, dst_ref=dst, send_sem=send, recv_sem=recv,
            device_id=device, device_id_type=pl.DeviceIdType.MESH,
        )

    barrier = pltpu.get_barrier_semaphore()
    phase = lax.rem(strip, 4)
    up_mutual, dn_mutual = jnp.logical_and(has_up, phase == 3), jnp.logical_and(has_dn, phase == 2)
    up_leads = jnp.logical_and(has_up, jnp.logical_or(phase == 1, phase == 2))
    dn_leads = jnp.logical_and(has_dn, phase == 3)
    up_follows = jnp.logical_and(has_up, phase == 0)
    dn_follows = jnp.logical_and(has_dn, phase < 2)

    def greet(exists, device):
        @pl.when(exists)
        def _():
            pl.semaphore_signal(
                barrier, inc=1, device_id=device, device_id_type=pl.DeviceIdType.MESH
            )

    def number(*conditions):
        return sum((x.astype(jnp.int32) for x in conditions), jnp.int32(0))

    greet(has_prev, prev_dev)
    greet(has_next, next_dev)
    far = [
        (jnp.logical_and(jnp.logical_or(is_first, is_last), far_next), {"sec": sec + GROUP}),
        (jnp.logical_and(jnp.logical_or(is_first, is_last), far_prev), {"sec": sec - GROUP}),
    ]
    if groups > 1:
        far.append((is_first, {"sec": sec + GROUP - 1}))
        far.append((is_last, {"sec": sec - GROUP + 1}))
    for exists, device in far:
        greet(exists, device)
    greet(up_mutual, up_dev)
    greet(dn_mutual, dn_dev)

    loads = [
        pltpu.make_async_copy(u_hbm, ub.at[0], local_sem.at[0]),
        pltpu.make_async_copy(c_hbm, cb, local_sem.at[1]),
        pltpu.make_async_copy(s_hbm, sho, local_sem.at[2]),
        pltpu.make_async_copy(w_hbm, wb, local_sem.at[3]),
    ]
    smalls = [
        pltpu.make_async_copy(class_hbm, class_k, local_sem.at[5]),
        pltpu.make_async_copy(cross_hbm, cross_k, local_sem.at[6]),
        pltpu.make_async_copy(fixed_hbm, fixed, local_sem.at[7]),
    ]
    for load in smalls + loads:
        load.start()

    chunks = [(i, p) for i in ORDER for p in range(PARTS)]
    relayed = [[(i, p) for i in RELAYED[step] for p in reversed(range(PARTS))] for step in range(2)]

    def source(step, first, i, p):
        src = u_hbm if step == 0 else ub.at[1]
        return src.at[first:first + 2, :, rows_of(i), span_of(p)]

    def to_prev(step, i, p):
        return remote(source(step, 0, i, p), nxt.at[step, :, :, rows_of(i), span_of(p)],
                      dn_send.at[step, i, p], dn_recv.at[step, i, p], prev_dev)

    def to_next(step, i, p):
        return remote(source(step, 1, i, p), prv.at[step, :, :, rows_of(i), span_of(p)],
                      up_send.at[step, i, p], up_recv.at[step, i, p], next_dev)

    def to_relay(step, i, p, up):
        return remote(source(step, 1 if up else 0, i, p), rel.at[step, i, p],
                      (up_send if up else dn_send).at[step, i, p], rel_recv.at[step, i, p],
                      {"sec": sec + GROUP if up else sec - GROUP})

    def from_relay(step, i, p, up):
        return remote(rel.at[step, i, p], (prv if up else nxt).at[step, :, :, rows_of(i), span_of(p)],
                      rel_send.at[step, i, p], (up_recv if up else dn_recv).at[step, i, p],
                      {"sec": sec - GROUP + 1 if up else sec + GROUP - 1})

    def by_relay(step, i, p, count):
        if (i, p) not in relayed[step]:
            return jnp.bool_(False)
        return relayed[step].index((i, p)) < PARTS * count

    def send_chunk(step, i, p):
        @pl.when(jnp.logical_and(has_prev, jnp.logical_not(by_relay(step, i, p, via_dn))))
        def _():
            to_prev(step, i, p).start()

        @pl.when(jnp.logical_and(has_next, jnp.logical_not(by_relay(step, i, p, via_up))))
        def _():
            to_next(step, i, p).start()

    def send_by_relay(step, i, p):
        if (i, p) in relayed[step]:
            @pl.when(by_relay(step, i, p, via_dn))
            def _():
                to_relay(step, i, p, False).start()

            @pl.when(by_relay(step, i, p, via_up))
            def _():
                to_relay(step, i, p, True).start()

    def forward_first(n):
        for count in range(n // PARTS + 1, len(RELAYED[0]) + 1):
            forward(0, *relayed[0][PARTS * count - 1 - n], relays == count)

    def forward(step, i, p, when=None):
        mine = by_relay(step, i, p, relays) if when is None else when

        @pl.when(mine)
        def _():
            to_relay(step, i, p, True).wait_recv()

        @pl.when(jnp.logical_and(mine, relay_up))
        def _():
            from_relay(step, i, p, True).start()

        @pl.when(jnp.logical_and(mine, relay_dn))
        def _():
            from_relay(step, i, p, False).start()

    def wait_chunk(step, i, p):
        @pl.when(has_next)
        def _():
            to_prev(step, i, p).wait_recv()

        @pl.when(has_prev)
        def _():
            to_next(step, i, p).wait_recv()

    def edge_to_dn(step):
        used = pl.ds(0, (3 if step == 0 else 2) * sections)
        return remote(edge_dn.at[step, used], edge_top.at[step, used],
                      edn_send.at[step], edn_recv.at[step], dn_dev)

    def edge_to_up(step):
        return remote(edge_up.at[step], edge_bot.at[step],
                      eup_send.at[step], eup_recv.at[step], up_dev)

    shifts_to_next = remote(s_hbm.at[1:3], shv, sh_send, sh_recv, next_dev)

    def stiffness(klass):
        table = [class_k[n] for n in range(CLASSES)]
        out = jnp.full(klass.shape, table[0], jnp.float32)
        for n in range(1, CLASSES):
            out = jnp.where(klass == n, table[n], out)
        return out

    def pack(step, last):
        dst, r = (edge_dn, rows - 1) if last else (edge_up, 0)
        for s in range(sections):
            for j in range(tiles):
                for c in range(2):
                    dst[step, 2 * s + c, pl.ds(j, 1), :] = ub[step, s, c, pl.ds(r, 1), pl.ds(j * LANES, LANES)]

    def send_edge(step, last, allowed):
        @pl.when(allowed)
        def _():
            (edge_to_dn if last else edge_to_up)(step).start()

    pl.semaphore_wait(
        barrier,
        number(has_prev, has_next, up_mutual, dn_mutual, up_leads, dn_leads, *(exists for exists, _ in far)),
    )
    send_chunk(0, *chunks[0])
    for chunk in chunks:
        send_by_relay(0, *chunk)
    for follows, leads, device in ((up_follows, up_leads, up_dev), (dn_follows, dn_leads, dn_dev)):
        greet(jnp.logical_or(follows, leads), device)

    @pl.when(has_next)
    def _():
        shifts_to_next.start()

    for load in smalls[:1] + loads[:2]:
        load.wait()
    pack(0, True)
    pack(0, False)
    for s in range(sections):
        for j in range(tiles):
            edge_class[s, pl.ds(j, 1), :] = cb[s, 1, pl.ds(rows - 1, 1), pl.ds(j * LANES, LANES)]
    for s in range(sections):
        edge_dn[0, 2 * sections + s] = stiffness(edge_class[s])

    send_edge(0, True, jnp.logical_or(dn_mutual, dn_leads))
    send_edge(0, False, jnp.logical_or(up_mutual, up_leads))
    for chunk in chunks[1:]:
        send_chunk(0, *chunk)

    @pl.when(jnp.logical_not(has_prev))
    def _():
        prv[...] = jnp.zeros_like(prv)
        for a in range(2):
            for h in range(2):
                for i in range(blocks):
                    for j in range(tiles):
                        shp[a, h, i, j] = 0

    @pl.when(jnp.logical_not(has_next))
    def _():
        nxt[...] = jnp.zeros_like(nxt)

    @pl.when(jnp.logical_not(has_up))
    def _():
        edge_top[...] = jnp.zeros_like(edge_top)

    @pl.when(jnp.logical_not(has_dn))
    def _():
        edge_bot[...] = jnp.zeros_like(edge_bot)

    def vertical(step):
        @pl.loop(0, tiles)
        def _(j):
            cols = cols_of(j)
            inside = jnp.logical_or(lane < LANES - 1, j < tiles - 1)
            for s in range(sections):
                u = [[ub[step, s, c, rows_of(i), cols] for c in range(2)] for i in range(blocks)]
                turned = [[pltpu.roll(x, BLOCK_ROWS - 1, 0) for x in pair] for pair in u]
                from_above = None
                for i in range(blocks):
                    if step == 0:
                        kh[s, rows_of(i), cols] = jnp.where(inside, stiffness(cb[s, 0, rows_of(i), cols]), 0.0)
                        k = stiffness(cb[s, 1, rows_of(i), cols])
                        if i == blocks - 1:
                            k = jnp.where(row < BLOCK_ROWS - 1, k, 0.0)
                        kv[s, rows_of(i), cols] = k
                    else:
                        k = kv[s, rows_of(i), cols]
                    e = []
                    for c in range(2):
                        below = turned[i][c]
                        if i < blocks - 1:
                            below = jnp.where(row == BLOCK_ROWS - 1, turned[i + 1][c], below)
                        e.append(below - u[i][c])
                    f = pulled(e[0], e[1], k)
                    down = [pltpu.roll(x, 1, 0) for x in f]
                    for c in range(2):
                        before = 0.0 if from_above is None else from_above[c]
                        pf[s, c, rows_of(i), cols] = f[c] - jnp.where(row == 0, before, down[c])
                    from_above = down

    def ahead(pair, o):
        return [pltpu.roll(x, (-o) & (LANES - 1), 1) for x in pair]

    def behind(pair, o):
        return [pltpu.roll(x, o & (LANES - 1), 1) for x in pair]

    def inner(step, i):
        here = rows_of(i)

        def tile(j, carry):
            cols, right_cols = cols_of(j), cols_of(jnp.minimum(j + 1, tiles - 1))
            ahead_left, flow_left = carry
            u = [[ub[step, s, c, here, cols] for c in range(2)] for s in range(sections)]
            force = [[pf[s, c, here, cols] for c in range(2)] for s in range(sections)]
            new_ahead, new_flow = [], []
            for s in range(sections):
                e = []
                for c in range(2):
                    coming = pltpu.roll(ub[step, s, c, here, right_cols], LANES - 1, 1)
                    new_ahead.append(coming)
                    e.append(jnp.where(lane == LANES - 1, coming, ahead_left[2 * s + c]) - u[s][c])
                f = pulled(e[0], e[1], kh[s, here, cols])
                for c in range(2):
                    turned = pltpu.roll(f[c], 1, 1)
                    new_flow.append(turned)
                    force[s][c] += f[c] - jnp.where(lane == 0, flow_left[2 * s + c], turned)
            for s, h, k in ((0, 1, k1), (1, 1, k1), (0, 2, k2)):
                o = sho[s, h - 1, i, j]
                there = ahead(u[s + h], o)
                f = pulled(there[0] - u[s][0], there[1] - u[s][1], k)
                back = behind(f, o)
                for c in range(2):
                    force[s][c] += f[c]
                    force[s + h][c] -= back[c]
            for s in range(sections):
                for c in range(2):
                    pf[s, c, here, cols] = force[s][c]
            return tuple(new_ahead), tuple(new_flow)

        start = (
            tuple(
                pltpu.roll(ub[step, s, c, here, pl.ds(0, LANES)], LANES - 1, 1)
                for s in range(sections)
                for c in range(2)
            ),
            tuple(jnp.zeros((BLOCK_ROWS, LANES), jnp.float32) for _ in range(2 * sections)),
        )
        lax.fori_loop(0, tiles, tile, start, unroll=min(UNROLL, tiles))

    def edge(step, last):
        if last:
            @pl.when(has_dn)
            def _():
                edge_to_up(step).wait_recv()
        else:
            @pl.when(has_up)
            def _():
                edge_to_dn(step).wait_recv()
        mine, theirs = (edge_dn, edge_bot) if last else (edge_up, edge_top)
        for s in range(sections):
            k = jnp.where(has_dn, edge_dn[0, 2 * sections + s], zero) if last else edge_top[0, 2 * sections + s]
            e = [theirs[step, 2 * s + c] - mine[step, 2 * s + c] for c in range(2)]
            f = pulled(e[0], e[1], k)
            for c in range(2):
                edge_flow[2 * s + c] = f[c]

    def outer(step, i, p):
        here = rows_of(i)
        edge_row = {0: 0, blocks - 1: BLOCK_ROWS - 1}.get(i)

        def tile(j, carry):
            cols = cols_of(j)
            u = [[ub[step, s, c, here, cols] for c in range(2)] for s in range(sections)]
            force = [[pf[s, c, here, cols] for c in range(2)] for s in range(sections)]
            if edge_row is not None:
                for s in range(sections):
                    for c in range(2):
                        f = jnp.broadcast_to(edge_flow[2 * s + c, pl.ds(j, 1), :], (BLOCK_ROWS, LANES))
                        force[s][c] += jnp.where(row == edge_row, f, 0.0)
            after = [[nxt[step, s, c, here, cols] for c in range(2)] for s in range(2)]
            for s, h, t, k in ((2, 1, 0, k1n), (1, 2, 0, k2n), (2, 2, 1, k2n)):
                there = ahead(after[t], sho[s, h - 1, i, j])
                f = pulled(there[0] - u[s][0], there[1] - u[s][1], k)
                for c in range(2):
                    force[s][c] += f[c]
            before = [[prv[step, s, c, here, cols] for c in range(2)] for s in range(2)]
            for t, h, s, k in ((1, 1, 0, k1p), (0, 2, 0, k2p), (1, 2, 1, k2p)):
                there = behind(before[t], shp[t, h - 1, i, j])
                f = pulled(there[0] - u[s][0], there[1] - u[s][1], k)
                for c in range(2):
                    force[s][c] += f[c]
            for s in range(sections):
                for c in range(2):
                    speed = (DAMPING * wb[s, c, here, cols] + TIME_STEP * force[s][c]) * moving[s]
                    moved = u[s][c] + TIME_STEP * speed
                    if step == 0:
                        wb[s, c, here, cols] = speed
                        ub[1, s, c, here, cols] = moved
                    else:
                        ow[s, c, here, cols] = speed
                        ou[s, c, here, cols] = moved
            return carry

        lax.fori_loop(p * tiles // PARTS, (p + 1) * tiles // PARTS, tile, 0, unroll=min(UNROLL, tiles // PARTS))

    for load in smalls[1:]:
        load.wait()
    k1, k2 = cross_k[0], cross_k[1]
    k1n, k2n = jnp.where(has_next, k1, zero), jnp.where(has_next, k2, zero)
    k1p, k2p = jnp.where(has_prev, k1, zero), jnp.where(has_prev, k2, zero)
    moving = [jnp.where(fixed[s] == 0, jnp.float32(1.0), zero) for s in range(sections)]

    def sent_chunk(step, i, p):
        @pl.when(has_prev)
        def _():
            to_prev(step, i, p).wait_send()

        @pl.when(has_next)
        def _():
            to_next(step, i, p).wait_send()

    def sent_before():
        for step in range(2):
            for chunk in relayed[step]:
                @pl.when(by_relay(step, *chunk, relays))
                def _():
                    from_relay(step, *chunk, True).wait_send()

            for chunk in chunks if step == 0 else chunks[:-PARTS]:
                sent_chunk(step, *chunk)

            @pl.when(has_dn)
            def _():
                edge_to_dn(step).wait_send()

            @pl.when(has_up)
            def _():
                edge_to_up(step).wait_send()

        @pl.when(has_next)
        def _():
            shifts_to_next.wait_send()

    for step in range(2):
        vertical(step)
        if step == 0:
            loads[2].wait()
        for n, i in enumerate(ORDER):
            inner(step, i)
            if step == 0 and n == 0:
                loads[3].wait()

                @pl.when(has_prev)
                def _():
                    shifts_to_next.wait_recv()
                    fetch = pltpu.make_async_copy(shv, shp, local_sem.at[4])
                    fetch.start()
                    fetch.wait()

            if i in (0, blocks - 1):
                edge(step, i != 0)
            if step == 1 and n == blocks - 1:
                sent_before()
            for p in range(PARTS):
                if step == 0 and n < 3:
                    m = n * PARTS + p
                    for k in (0, 1) if m == 0 else (m + 1,):
                        if k < PARTS * len(RELAYED[0]):
                            forward_first(k)
                elif step == 0 and n == 3:
                    forward(1, RELAYED[1][0], p)
                elif step == 1 and n == 0:
                    forward(1, RELAYED[1][2], p)
                wait_chunk(step, i, p)
                outer(step, i, p)
                if step == 0:
                    send_by_relay(1, i, p)
                    if n == 3:
                        send_chunk(1, i, p)
            if step == 0:
                if n == 0:
                    @pl.when(jnp.logical_or(up_follows, dn_follows))
                    def _():
                        pl.semaphore_wait(barrier, number(up_follows, dn_follows))

                    send_edge(0, True, dn_follows)
                    send_edge(0, False, up_follows)
                if i in (0, blocks - 1):
                    pack(1, i != 0)
                    send_edge(1, i != 0, has_dn if i else has_up)
                if n == 1:
                    for chunk in chunks[:PARTS]:
                        send_chunk(1, *chunk)
                elif n == 2:
                    for chunk in chunks[PARTS:3 * PARTS]:
                        send_chunk(1, *chunk)
                    for p in range(PARTS):
                        forward(1, RELAYED[1][1], p)

    for chunk in chunks[-PARTS:]:
        sent_chunk(1, *chunk)


def store(ou, ow, pos, vel, sem):
    copies = []
    for k, (src, dst) in enumerate(((ou, pos), (ow, vel))):
        for s in range(src.shape[0]):
            copies.append(pltpu.make_async_copy(src.at[s], dst.at[s], sem.at[k, s]))
    for copy in copies:
        copy.start()
    for copy in copies:
        copy.wait()


def per_device(positions, velocity, spring_class, match_shift, fixed, class_stiffness, cross_stiffness):
    sections, comps, rows, width = positions.shape
    blocks, tiles = rows // BLOCK_ROWS, width // LANES
    full = (sections, comps, rows, width)
    f32, i32 = jnp.float32, jnp.int32
    any_spec = pl.BlockSpec(memory_space=pl.ANY)
    smem_spec = pl.BlockSpec(memory_space=pltpu.SMEM)
    vmem_spec = pl.BlockSpec(memory_space=pltpu.VMEM)
    dma = pltpu.SemaphoreType.DMA
    moved, speed = pl.pallas_call(
        kernel,
        out_shape=(pltpu.VMEM(full, f32), pltpu.VMEM(full, f32)),
        in_specs=[any_spec] * 7,
        out_specs=(vmem_spec, vmem_spec),
        scratch_shapes=[
            pltpu.SMEM((sections,), i32), pltpu.SMEM((CLASSES,), f32), pltpu.SMEM((2,), f32),
            pltpu.VMEM((2,) + full, f32),
            pltpu.VMEM(full, f32),
            pltpu.VMEM(full, i32),
            pltpu.VMEM((sections, rows, width), f32),
            pltpu.VMEM((sections, rows, width), f32),
            pltpu.VMEM(full, f32),
            pltpu.VMEM((2, 2, comps, rows, width), f32),
            pltpu.VMEM((2, 2, comps, rows, width), f32),
            pltpu.VMEM((2, blocks, PARTS, 2, comps, BLOCK_ROWS, width // PARTS), f32),
            pltpu.VMEM((2, 3 * sections, tiles, LANES), f32),
            pltpu.VMEM((2, 2 * sections, tiles, LANES), f32),
            pltpu.VMEM((2, 3 * sections, tiles, LANES), f32),
            pltpu.VMEM((2, 2 * sections, tiles, LANES), f32),
            pltpu.VMEM((sections, tiles, LANES), i32),
            pltpu.VMEM((2 * sections, tiles, LANES), f32),
            pltpu.VMEM((2, 2, blocks, tiles), i32),
            pltpu.SMEM((2, 2, blocks, tiles), i32),
            pltpu.SMEM((sections, 2, blocks, tiles), i32),
            dma((8,)),
            *[dma((2, blocks, PARTS)) for _ in range(6)],
            dma((2,)), dma((2,)), dma((2,)), dma((2,)), dma(()), dma(()),
        ],
        compiler_params=pltpu.CompilerParams(collective_id=0, has_side_effects=True),
        name="relax",
    )(positions, velocity, spring_class, match_shift, fixed, class_stiffness, cross_stiffness)
    moved = pltpu.with_memory_space_constraint(moved, pltpu.VMEM)
    speed = pltpu.with_memory_space_constraint(speed, pltpu.VMEM)
    return pl.pallas_call(
        store,
        out_shape=(jax.ShapeDtypeStruct(full, f32), jax.ShapeDtypeStruct(full, f32)),
        in_specs=[vmem_spec] * 2,
        out_specs=(any_spec, any_spec),
        scratch_shapes=[dma((2, sections))],
        name="store",
    )(moved, speed)


def solution(mesh):
    grid = P("sec", None, "strip", None)
    return jax.shard_map(
        per_device,
        mesh=mesh,
        in_specs=(grid, grid, grid, grid, P("sec"), P(), P()),
        out_specs=(grid, grid),
        check_vma=False,
    )
```

```python
import jax
import jax.numpy as jnp
from jax import lax
from jax.experimental import pallas as pl
from jax.experimental.pallas import tpu as pltpu
from jax.sharding import PartitionSpec as P

BLOCK_ROWS = 8
LANES = 128
CLASSES = 8
DAMPING = 0.9
TIME_STEP = 0.35
ORDER = (1, 3, 0, 2)
RELAYED = ((2, 0, 3), (3, 1, 0))
PARTS = 2
GROUP = 4
UNROLL = 4


def pulled(ex, ey, k):
    r = 1.0 / (1.0 + (ex * ex + ey * ey))
    g = k * (1.5 - 0.5 * r)
    return ex * g, ey * g


def kernel(
    u_hbm, w_hbm, c_hbm, s_hbm, fixed_hbm, class_hbm, cross_hbm, ou, ow, fixed, class_k, cross_k,
    ub, wb, cb, kh, kv, pf, nxt, prv, rel,
    edge_dn, edge_up, edge_top, edge_bot, edge_class, edge_flow, shv, shp, sho,
    local_sem, dn_send, dn_recv, up_send, up_recv,
    rel_send, rel_recv, edn_send, edn_recv, eup_send, eup_recv, sh_send, sh_recv,
):
    n_sec, n_strip = lax.axis_size("sec"), lax.axis_size("strip")
    sec, strip = lax.axis_index("sec"), lax.axis_index("strip")
    has_prev, has_next = sec > 0, sec < n_sec - 1
    has_up, has_dn = strip > 0, strip < n_strip - 1
    prev_dev, next_dev = {"sec": sec - 1}, {"sec": sec + 1}
    up_dev, dn_dev = {"strip": strip - 1}, {"strip": strip + 1}
    groups, group = n_sec // GROUP, sec // GROUP
    is_first = jnp.logical_and(lax.rem(sec, GROUP) == 0, group < groups)
    is_last = lax.rem(sec, GROUP) == GROUP - 1
    far_next, far_prev = sec + GROUP < groups * GROUP, sec >= GROUP
    via_up = jnp.where(jnp.logical_and(is_last, far_next), group + 1, 0)
    via_dn = jnp.where(jnp.logical_and(is_first, far_prev), groups - group, 0)
    relay_up, relay_dn = jnp.logical_and(is_last, far_prev), jnp.logical_and(is_first, far_next)
    relays = jnp.where(relay_up, group, jnp.where(relay_dn, groups - 1 - group, 0))
    sections, _, rows, width = u_hbm.shape
    blocks, tiles = rows // BLOCK_ROWS, width // LANES
    lane = lax.broadcasted_iota(jnp.int32, (BLOCK_ROWS, LANES), 1)
    row = lax.broadcasted_iota(jnp.int32, (BLOCK_ROWS, LANES), 0)
    zero = jnp.float32(0.0)

    def rows_of(i):
        return pl.ds(BLOCK_ROWS * i, BLOCK_ROWS)

    def span_of(p):
        return pl.ds(p * (width // PARTS), width // PARTS)

    def cols_of(j):
        return pl.ds(pl.multiple_of(j * LANES, LANES), LANES)

    def remote(src, dst, send, recv, device):
        return pltpu.make_async_remote_copy(
            src_ref=src, dst_ref=dst, send_sem=send, recv_sem=recv,
            device_id=device, device_id_type=pl.DeviceIdType.MESH,
        )

    barrier = pltpu.get_barrier_semaphore()
    phase = lax.rem(strip, 4)
    up_mutual, dn_mutual = jnp.logical_and(has_up, phase == 3), jnp.logical_and(has_dn, phase == 2)
    up_leads = jnp.logical_and(has_up, jnp.logical_or(phase == 1, phase == 2))
    dn_leads = jnp.logical_and(has_dn, phase == 3)
    up_follows = jnp.logical_and(has_up, phase == 0)
    dn_follows = jnp.logical_and(has_dn, phase < 2)

    def greet(exists, device):
        @pl.when(exists)
        def _():
            pl.semaphore_signal(
                barrier, inc=1, device_id=device, device_id_type=pl.DeviceIdType.MESH
            )

    def number(*conditions):
        return sum((x.astype(jnp.int32) for x in conditions), jnp.int32(0))

    greet(has_prev, prev_dev)
    greet(has_next, next_dev)
    far = [
        (jnp.logical_and(jnp.logical_or(is_first, is_last), far_next), {"sec": sec + GROUP}),
        (jnp.logical_and(jnp.logical_or(is_first, is_last), far_prev), {"sec": sec - GROUP}),
    ]
    if groups > 1:
        far.append((is_first, {"sec": sec + GROUP - 1}))
        far.append((is_last, {"sec": sec - GROUP + 1}))
    for exists, device in far:
        greet(exists, device)
    greet(up_mutual, up_dev)
    greet(dn_mutual, dn_dev)

    loads = [
        pltpu.make_async_copy(u_hbm, ub.at[0], local_sem.at[0]),
        pltpu.make_async_copy(c_hbm, cb, local_sem.at[1]),
        pltpu.make_async_copy(s_hbm, sho, local_sem.at[2]),
        pltpu.make_async_copy(w_hbm, wb, local_sem.at[3]),
    ]
    smalls = [
        pltpu.make_async_copy(class_hbm, class_k, local_sem.at[5]),
        pltpu.make_async_copy(cross_hbm, cross_k, local_sem.at[6]),
        pltpu.make_async_copy(fixed_hbm, fixed, local_sem.at[7]),
    ]
    for load in smalls + loads:
        load.start()

    chunks = [(i, p) for i in ORDER for p in range(PARTS)]
    relayed = [[(i, p) for i in RELAYED[step] for p in reversed(range(PARTS))] for step in range(2)]

    def source(step, first, i, p):
        src = u_hbm if step == 0 else ub.at[1]
        return src.at[first:first + 2, :, rows_of(i), span_of(p)]

    def to_prev(step, i, p):
        return remote(source(step, 0, i, p), nxt.at[step, :, :, rows_of(i), span_of(p)],
                      dn_send.at[step, i, p], dn_recv.at[step, i, p], prev_dev)

    def to_next(step, i, p):
        return remote(source(step, 1, i, p), prv.at[step, :, :, rows_of(i), span_of(p)],
                      up_send.at[step, i, p], up_recv.at[step, i, p], next_dev)

    def to_relay(step, i, p, up):
        return remote(source(step, 1 if up else 0, i, p), rel.at[step, i, p],
                      (up_send if up else dn_send).at[step, i, p], rel_recv.at[step, i, p],
                      {"sec": sec + GROUP if up else sec - GROUP})

    def from_relay(step, i, p, up):
        return remote(rel.at[step, i, p], (prv if up else nxt).at[step, :, :, rows_of(i), span_of(p)],
                      rel_send.at[step, i, p], (up_recv if up else dn_recv).at[step, i, p],
                      {"sec": sec - GROUP + 1 if up else sec + GROUP - 1})

    def by_relay(step, i, p, count):
        if (i, p) not in relayed[step]:
            return jnp.bool_(False)
        return relayed[step].index((i, p)) < PARTS * count

    def send_chunk(step, i, p):
        @pl.when(jnp.logical_and(has_prev, jnp.logical_not(by_relay(step, i, p, via_dn))))
        def _():
            to_prev(step, i, p).start()

        @pl.when(jnp.logical_and(has_next, jnp.logical_not(by_relay(step, i, p, via_up))))
        def _():
            to_next(step, i, p).start()

    def send_by_relay(step, i, p):
        if (i, p) in relayed[step]:
            @pl.when(by_relay(step, i, p, via_dn))
            def _():
                to_relay(step, i, p, False).start()

            @pl.when(by_relay(step, i, p, via_up))
            def _():
                to_relay(step, i, p, True).start()

    def forward_first(n):
        for count in range(n // PARTS + 1, len(RELAYED[0]) + 1):
            forward(0, *relayed[0][PARTS * count - 1 - n], relays == count)

    def forward(step, i, p, when=None):
        mine = by_relay(step, i, p, relays) if when is None else when

        @pl.when(mine)
        def _():
            to_relay(step, i, p, True).wait_recv()

        @pl.when(jnp.logical_and(mine, relay_up))
        def _():
            from_relay(step, i, p, True).start()

        @pl.when(jnp.logical_and(mine, relay_dn))
        def _():
            from_relay(step, i, p, False).start()

    def wait_chunk(step, i, p):
        @pl.when(has_next)
        def _():
            to_prev(step, i, p).wait_recv()

        @pl.when(has_prev)
        def _():
            to_next(step, i, p).wait_recv()

    def edge_to_dn(step):
        used = pl.ds(0, (3 if step == 0 else 2) * sections)
        return remote(edge_dn.at[step, used], edge_top.at[step, used],
                      edn_send.at[step], edn_recv.at[step], dn_dev)

    def edge_to_up(step):
        return remote(edge_up.at[step], edge_bot.at[step],
                      eup_send.at[step], eup_recv.at[step], up_dev)

    shifts_to_next = remote(s_hbm.at[1:3], shv, sh_send, sh_recv, next_dev)

    def stiffness(klass):
        table = [class_k[n] for n in range(CLASSES)]
        out = jnp.full(klass.shape, table[0], jnp.float32)
        for n in range(1, CLASSES):
            out = jnp.where(klass == n, table[n], out)
        return out

    def pack(step, last):
        dst, r = (edge_dn, rows - 1) if last else (edge_up, 0)
        for s in range(sections):
            for j in range(tiles):
                for c in range(2):
                    dst[step, 2 * s + c, pl.ds(j, 1), :] = ub[step, s, c, pl.ds(r, 1), pl.ds(j * LANES, LANES)]

    def send_edge(step, last, allowed):
        @pl.when(allowed)
        def _():
            (edge_to_dn if last else edge_to_up)(step).start()

    pl.semaphore_wait(
        barrier,
        number(has_prev, has_next, up_mutual, dn_mutual, up_leads, dn_leads, *(exists for exists, _ in far)),
    )
    send_chunk(0, *chunks[0])
    for chunk in chunks:
        send_by_relay(0, *chunk)
    for follows, leads, device in ((up_follows, up_leads, up_dev), (dn_follows, dn_leads, dn_dev)):
        greet(jnp.logical_or(follows, leads), device)

    @pl.when(has_next)
    def _():
        shifts_to_next.start()

    for load in smalls[:1] + loads[:2]:
        load.wait()
    pack(0, True)
    pack(0, False)
    for s in range(sections):
        for j in range(tiles):
            edge_class[s, pl.ds(j, 1), :] = cb[s, 1, pl.ds(rows - 1, 1), pl.ds(j * LANES, LANES)]
    for s in range(sections):
        edge_dn[0, 2 * sections + s] = stiffness(edge_class[s])

    send_edge(0, True, jnp.logical_or(dn_mutual, dn_leads))
    send_edge(0, False, jnp.logical_or(up_mutual, up_leads))
    for chunk in chunks[1:]:
        send_chunk(0, *chunk)

    @pl.when(jnp.logical_not(has_prev))
    def _():
        prv[...] = jnp.zeros_like(prv)
        for a in range(2):
            for h in range(2):
                for i in range(blocks):
                    for j in range(tiles):
                        shp[a, h, i, j] = 0

    @pl.when(jnp.logical_not(has_next))
    def _():
        nxt[...] = jnp.zeros_like(nxt)

    @pl.when(jnp.logical_not(has_up))
    def _():
        edge_top[...] = jnp.zeros_like(edge_top)

    @pl.when(jnp.logical_not(has_dn))
    def _():
        edge_bot[...] = jnp.zeros_like(edge_bot)

    def vertical(step):
        @pl.loop(0, tiles)
        def _(j):
            cols = cols_of(j)
            inside = jnp.logical_or(lane < LANES - 1, j < tiles - 1)
            for s in range(sections):
                u = [[ub[step, s, c, rows_of(i), cols] for c in range(2)] for i in range(blocks)]
                turned = [[pltpu.roll(x, BLOCK_ROWS - 1, 0) for x in pair] for pair in u]
                from_above = None
                for i in range(blocks):
                    if step == 0:
                        kh[s, rows_of(i), cols] = jnp.where(inside, stiffness(cb[s, 0, rows_of(i), cols]), 0.0)
                        k = stiffness(cb[s, 1, rows_of(i), cols])
                        if i == blocks - 1:
                            k = jnp.where(row < BLOCK_ROWS - 1, k, 0.0)
                        kv[s, rows_of(i), cols] = k
                    else:
                        k = kv[s, rows_of(i), cols]
                    e = []
                    for c in range(2):
                        below = turned[i][c]
                        if i < blocks - 1:
                            below = jnp.where(row == BLOCK_ROWS - 1, turned[i + 1][c], below)
                        e.append(below - u[i][c])
                    f = pulled(e[0], e[1], k)
                    down = [pltpu.roll(x, 1, 0) for x in f]
                    for c in range(2):
                        before = 0.0 if from_above is None else from_above[c]
                        pf[s, c, rows_of(i), cols] = f[c] - jnp.where(row == 0, before, down[c])
                    from_above = down

    def ahead(pair, o):
        return [pltpu.roll(x, (-o) & (LANES - 1), 1) for x in pair]

    def behind(pair, o):
        return [pltpu.roll(x, o & (LANES - 1), 1) for x in pair]

    def inner(step, i):
        here = rows_of(i)

        def tile(j, carry):
            cols, right_cols = cols_of(j), cols_of(jnp.minimum(j + 1, tiles - 1))
            ahead_left, flow_left = carry
            u = [[ub[step, s, c, here, cols] for c in range(2)] for s in range(sections)]
            force = [[pf[s, c, here, cols] for c in range(2)] for s in range(sections)]
            new_ahead, new_flow = [], []
            for s in range(sections):
                e = []
                for c in range(2):
                    coming = pltpu.roll(ub[step, s, c, here, right_cols], LANES - 1, 1)
                    new_ahead.append(coming)
                    e.append(jnp.where(lane == LANES - 1, coming, ahead_left[2 * s + c]) - u[s][c])
                f = pulled(e[0], e[1], kh[s, here, cols])
                for c in range(2):
                    turned = pltpu.roll(f[c], 1, 1)
                    new_flow.append(turned)
                    force[s][c] += f[c] - jnp.where(lane == 0, flow_left[2 * s + c], turned)
            for s, h, k in ((0, 1, k1), (1, 1, k1), (0, 2, k2)):
                o = sho[s, h - 1, i, j]
                there = ahead(u[s + h], o)
                f = pulled(there[0] - u[s][0], there[1] - u[s][1], k)
                back = behind(f, o)
                for c in range(2):
                    force[s][c] += f[c]
                    force[s + h][c] -= back[c]
            for s in range(sections):
                for c in range(2):
                    pf[s, c, here, cols] = force[s][c]
            return tuple(new_ahead), tuple(new_flow)

        start = (
            tuple(
                pltpu.roll(ub[step, s, c, here, pl.ds(0, LANES)], LANES - 1, 1)
                for s in range(sections)
                for c in range(2)
            ),
            tuple(jnp.zeros((BLOCK_ROWS, LANES), jnp.float32) for _ in range(2 * sections)),
        )
        lax.fori_loop(0, tiles, tile, start, unroll=min(UNROLL, tiles))

    def edge(step, last):
        if last:
            @pl.when(has_dn)
            def _():
                edge_to_up(step).wait_recv()
        else:
            @pl.when(has_up)
            def _():
                edge_to_dn(step).wait_recv()
        mine, theirs = (edge_dn, edge_bot) if last else (edge_up, edge_top)
        for s in range(sections):
            k = jnp.where(has_dn, edge_dn[0, 2 * sections + s], zero) if last else edge_top[0, 2 * sections + s]
            e = [theirs[step, 2 * s + c] - mine[step, 2 * s + c] for c in range(2)]
            f = pulled(e[0], e[1], k)
            for c in range(2):
                edge_flow[2 * s + c] = f[c]

    def outer(step, i, p):
        here = rows_of(i)
        edge_row = {0: 0, blocks - 1: BLOCK_ROWS - 1}.get(i)

        def tile(j, carry):
            cols = cols_of(j)
            u = [[ub[step, s, c, here, cols] for c in range(2)] for s in range(sections)]
            force = [[pf[s, c, here, cols] for c in range(2)] for s in range(sections)]
            if edge_row is not None:
                for s in range(sections):
                    for c in range(2):
                        f = jnp.broadcast_to(edge_flow[2 * s + c, pl.ds(j, 1), :], (BLOCK_ROWS, LANES))
                        force[s][c] += jnp.where(row == edge_row, f, 0.0)
            after = [[nxt[step, s, c, here, cols] for c in range(2)] for s in range(2)]
            for s, h, t, k in ((2, 1, 0, k1n), (1, 2, 0, k2n), (2, 2, 1, k2n)):
                there = ahead(after[t], sho[s, h - 1, i, j])
                f = pulled(there[0] - u[s][0], there[1] - u[s][1], k)
                for c in range(2):
                    force[s][c] += f[c]
            before = [[prv[step, s, c, here, cols] for c in range(2)] for s in range(2)]
            for t, h, s, k in ((1, 1, 0, k1p), (0, 2, 0, k2p), (1, 2, 1, k2p)):
                there = behind(before[t], shp[t, h - 1, i, j])
                f = pulled(there[0] - u[s][0], there[1] - u[s][1], k)
                for c in range(2):
                    force[s][c] += f[c]
            for s in range(sections):
                for c in range(2):
                    speed = (DAMPING * wb[s, c, here, cols] + TIME_STEP * force[s][c]) * moving[s]
                    moved = u[s][c] + TIME_STEP * speed
                    if step == 0:
                        wb[s, c, here, cols] = speed
                        ub[1, s, c, here, cols] = moved
                    else:
                        ow[s, c, here, cols] = speed
                        ou[s, c, here, cols] = moved
            return carry

        lax.fori_loop(p * tiles // PARTS, (p + 1) * tiles // PARTS, tile, 0, unroll=min(UNROLL, tiles // PARTS))

    for load in smalls[1:]:
        load.wait()
    k1, k2 = cross_k[0], cross_k[1]
    k1n, k2n = jnp.where(has_next, k1, zero), jnp.where(has_next, k2, zero)
    k1p, k2p = jnp.where(has_prev, k1, zero), jnp.where(has_prev, k2, zero)
    moving = [jnp.where(fixed[s] == 0, jnp.float32(1.0), zero) for s in range(sections)]

    def sent_chunk(step, i, p):
        @pl.when(has_prev)
        def _():
            to_prev(step, i, p).wait_send()

        @pl.when(has_next)
        def _():
            to_next(step, i, p).wait_send()

    def sent_before():
        for step in range(2):
            for chunk in relayed[step]:
                @pl.when(by_relay(step, *chunk, relays))
                def _():
                    from_relay(step, *chunk, True).wait_send()

            for chunk in chunks if step == 0 else chunks[:-PARTS]:
                sent_chunk(step, *chunk)

            @pl.when(has_dn)
            def _():
                edge_to_dn(step).wait_send()

            @pl.when(has_up)
            def _():
                edge_to_up(step).wait_send()

        @pl.when(has_next)
        def _():
            shifts_to_next.wait_send()

    for step in range(2):
        vertical(step)
        if step == 0:
            loads[2].wait()
        for n, i in enumerate(ORDER):
            inner(step, i)
            if step == 0 and n == 0:
                loads[3].wait()

                @pl.when(has_prev)
                def _():
                    shifts_to_next.wait_recv()
                    fetch = pltpu.make_async_copy(shv, shp, local_sem.at[4])
                    fetch.start()
                    fetch.wait()

            if i in (0, blocks - 1):
                edge(step, i != 0)
            if step == 1 and n == blocks - 1:
                sent_before()
            for p in range(PARTS):
                if step == 0 and n < 3:
                    m = n * PARTS + p
                    for k in (0, 1) if m == 0 else (m + 1,):
                        if k < PARTS * len(RELAYED[0]):
                            forward_first(k)
                elif step == 0 and n == 3:
                    forward(1, RELAYED[1][0], p)
                elif step == 1 and n == 0:
                    forward(1, RELAYED[1][2], p)
                wait_chunk(step, i, p)
                outer(step, i, p)
                if step == 0:
                    send_by_relay(1, i, p)
                    if n == 3:
                        send_chunk(1, i, p)
            if step == 0:
                if n == 0:
                    @pl.when(jnp.logical_or(up_follows, dn_follows))
                    def _():
                        pl.semaphore_wait(barrier, number(up_follows, dn_follows))

                    send_edge(0, True, dn_follows)
                    send_edge(0, False, up_follows)
                if i in (0, blocks - 1):
                    pack(1, i != 0)
                    send_edge(1, i != 0, has_dn if i else has_up)
                if n == 1:
                    for chunk in chunks[:PARTS]:
                        send_chunk(1, *chunk)
                elif n == 2:
                    for chunk in chunks[PARTS:3 * PARTS]:
                        send_chunk(1, *chunk)
                    for p in range(PARTS):
                        forward(1, RELAYED[1][1], p)

    for chunk in chunks[-PARTS:]:
        sent_chunk(1, *chunk)


def store(ou, ow, pos, vel, sem):
    copies = []
    for k, (src, dst) in enumerate(((ou, pos), (ow, vel))):
        copies.append(pltpu.make_async_copy(src, dst, sem.at[k]))
    for copy in copies:
        copy.start()
    for copy in copies:
        copy.wait()


def per_device(positions, velocity, spring_class, match_shift, fixed, class_stiffness, cross_stiffness):
    sections, comps, rows, width = positions.shape
    blocks, tiles = rows // BLOCK_ROWS, width // LANES
    full = (sections, comps, rows, width)
    f32, i32 = jnp.float32, jnp.int32
    any_spec = pl.BlockSpec(memory_space=pl.ANY)
    smem_spec = pl.BlockSpec(memory_space=pltpu.SMEM)
    vmem_spec = pl.BlockSpec(memory_space=pltpu.VMEM)
    dma = pltpu.SemaphoreType.DMA
    moved, speed = pl.pallas_call(
        kernel,
        out_shape=(pltpu.VMEM(full, f32), pltpu.VMEM(full, f32)),
        in_specs=[any_spec] * 7,
        out_specs=(vmem_spec, vmem_spec),
        scratch_shapes=[
            pltpu.SMEM((sections,), i32), pltpu.SMEM((CLASSES,), f32), pltpu.SMEM((2,), f32),
            pltpu.VMEM((2,) + full, f32),
            pltpu.VMEM(full, f32),
            pltpu.VMEM(full, i32),
            pltpu.VMEM((sections, rows, width), f32),
            pltpu.VMEM((sections, rows, width), f32),
            pltpu.VMEM(full, f32),
            pltpu.VMEM((2, 2, comps, rows, width), f32),
            pltpu.VMEM((2, 2, comps, rows, width), f32),
            pltpu.VMEM((2, blocks, PARTS, 2, comps, BLOCK_ROWS, width // PARTS), f32),
            pltpu.VMEM((2, 3 * sections, tiles, LANES), f32),
            pltpu.VMEM((2, 2 * sections, tiles, LANES), f32),
            pltpu.VMEM((2, 3 * sections, tiles, LANES), f32),
            pltpu.VMEM((2, 2 * sections, tiles, LANES), f32),
            pltpu.VMEM((sections, tiles, LANES), i32),
            pltpu.VMEM((2 * sections, tiles, LANES), f32),
            pltpu.VMEM((2, 2, blocks, tiles), i32),
            pltpu.SMEM((2, 2, blocks, tiles), i32),
            pltpu.SMEM((sections, 2, blocks, tiles), i32),
            dma((8,)),
            *[dma((2, blocks, PARTS)) for _ in range(6)],
            dma((2,)), dma((2,)), dma((2,)), dma((2,)), dma(()), dma(()),
        ],
        compiler_params=pltpu.CompilerParams(collective_id=0, has_side_effects=True),
        name="relax",
    )(positions, velocity, spring_class, match_shift, fixed, class_stiffness, cross_stiffness)
    moved = pltpu.with_memory_space_constraint(moved, pltpu.VMEM)
    speed = pltpu.with_memory_space_constraint(speed, pltpu.VMEM)
    return pl.pallas_call(
        store,
        out_shape=(jax.ShapeDtypeStruct(full, f32), jax.ShapeDtypeStruct(full, f32)),
        in_specs=[vmem_spec] * 2,
        out_specs=(any_spec, any_spec),
        scratch_shapes=[dma((2,))],
        name="store",
    )(moved, speed)


def solution(mesh):
    grid = P("sec", None, "strip", None)
    return jax.shard_map(
        per_device,
        mesh=mesh,
        in_specs=(grid, grid, grid, grid, P("sec"), P(), P()),
        out_specs=(grid, grid),
        check_vma=False,
    )
```
